512 devices in a mesh: row: 64 (over z, y), col: 8 (over x, core).
Axes of the slice: x: 4, y: 4, z: 16, core: 2. Of those that a mesh axis runs over, the one named last changes fastest.
Arguments:
- traces: float32 [16, 32768], P('col', 'row'), may hold values from -50 to 50
Outputs:
- overwritten: float32 [32768, 4096], P('row', 'col')
- coupling: float32 [256, 4096], P(None, 'col')
The draws below stay inside these ranges and needn't reach their ends.
All inputs are finite; a program needn't handle non-finite values.
Results may differ from the reference program's by a relative error of at most 0.0015.
Values sent between devices are 32-bit elements; how exact they have to be, the bound alone decides.
A program may use at most 64 MiB of HBM per device.

```python
import math
import jax
import jax.numpy as jnp
from jax import lax

CH = 16
TAPS = 256
ROWS = 32768
WIDE = 256


def draw_traces(key, part):
    subkeys = jax.random.split(key, 4)
    gains = jnp.exp(jax.random.uniform(subkeys[0], (CH, 1), jnp.float32, math.log(0.5), math.log(2.0)))
    roughness = jnp.exp(jax.random.uniform(subkeys[1], (CH, ROWS), jnp.float32, math.log(0.5), math.log(2.0)))
    timeline = jnp.arange(ROWS, dtype=jnp.float32) / ROWS
    envelope = 0.5 + timeline
    own_noise = jax.random.truncated_normal(subkeys[2], -5.0, 5.0, (CH, ROWS + 1), jnp.float32)
    common = jax.random.truncated_normal(subkeys[3], -5.0, 5.0, (1, ROWS), jnp.float32)
    shared = 0.6
    separate = 0.6
    filtered = own_noise[:, 1:] + 0.7 * own_noise[:, :-1]
    return gains * envelope[None, :] * roughness * (shared * common + separate * filtered)


def setup_inputs(seed: int = 0) -> dict:
    arg_keys = jax.random.split(jax.random.key(seed), 2)
    return {
        "traces": draw_traces(jax.random.fold_in(arg_keys[1], 71), 0),
    }


def trace_matrix(samples, offsets):
    padded = jnp.concatenate([jnp.zeros((TAPS,), jnp.float32), samples])
    return padded[offsets]

def reference(traces):
    highest = lax.Precision.HIGHEST
    offsets = (jnp.arange(ROWS)[:, None] - jnp.arange(TAPS)[None, :] + TAPS).astype(jnp.int32)
    panel_cols = trace_matrix(traces[0], offsets)[:, :WIDE]
    gram_sum = jnp.dot(panel_cols.T, panel_cols, precision=highest) / ROWS
    factor_low = jnp.linalg.cholesky(gram_sum)
    inverse = jax.scipy.linalg.solve_triangular(factor_low, jnp.eye(WIDE, dtype=jnp.float32), lower=True)
    basis_cols = jnp.dot(panel_cols, inverse.T, precision=highest)

    def one_trace(samples):
        blocked = trace_matrix(samples, offsets)
        coupled = jnp.dot(inverse, jnp.dot(panel_cols.T, blocked, precision=highest) / ROWS, precision=highest)
        return (coupled, blocked - jnp.dot(basis_cols, coupled, precision=highest))
    coupled, remainder = lax.map(one_trace, traces)
    coupling = jnp.transpose(coupled, (1, 0, 2)).reshape(WIDE, CH * TAPS)
    overwritten = jnp.transpose(remainder, (1, 0, 2)).reshape(ROWS, CH * TAPS)
    overwritten = overwritten.at[:, :WIDE].set(basis_cols)
    return (overwritten, coupling)
```

```python
import functools

import jax
import jax.numpy as jnp
from jax import lax
from jax.experimental import pallas as pl
from jax.experimental.pallas import tpu as pltpu
from jax.sharding import PartitionSpec as P

TAPS = 256
WIDE = 256
SLAB = 4
MESH = pl.DeviceIdType.MESH
HIGHEST = lax.Precision.HIGHEST
VM = pl.BlockSpec(memory_space=pltpu.VMEM)


def dot(a, b, da=1, db=0):
    return lax.dot_general(
        a, b, (((da,), (db,)), ((), ())), precision=HIGHEST, preferred_element_type=jnp.float32
    )


def iota(shape, axis):
    return lax.broadcasted_iota(jnp.int32, shape, axis)


def anti_identity():
    return jnp.where(iota((128, 128), 0) + iota((128, 128), 1) == 127, 1.0, 0.0).astype(jnp.float32)


def lag_kernel(
    slabs, cols,
    x_ref, sums_ref, ext_ref, tail_ref,
    own0, slab0, slabc, before0, after0, beforec, tail0, tailc, lags,
    local_sem, send_x, recv_x, send_0, recv_0, send_hc, recv_hc,
    send_s0, recv_s0, send_hb, recv_hb, send_ha, recv_ha, send_t, recv_t, send_l, recv_l,
):
    row, col = lax.axis_index("row"), lax.axis_index("col")
    z, y = row // SLAB, row % SLAB
    rows = x_ref.shape[1]
    cut = rows - TAPS
    first, last = y == 0, y == SLAB - 1
    has_before, has_after = z > 0, z < slabs - 1
    in_tail = z == slabs - 1

    def at(zz, yy, cc):
        return (zz * SLAB + yy, cc)

    def remote(src, dst, send, recv, where):
        return pltpu.make_async_remote_copy(
            src_ref=src, dst_ref=dst, send_sem=send, recv_sem=recv, device_id=where, device_id_type=MESH
        )

    barrier = pltpu.get_barrier_semaphore()

    def greet(where):
        pl.semaphore_signal(barrier, inc=1, device_id=where, device_id_type=MESH)

    @pl.loop(1, slabs)
    def _(k):
        greet(at((z + k) % slabs, y, col))

    for k in range(1, SLAB):
        greet(at(z, (y + k) % SLAB, col))

    @pl.when(col == 0)
    def _():
        for k in range(1, cols):
            greet(at(z, y, k))

    @pl.when(col != 0)
    def _():
        greet(at(z, y, 0))

    @pl.when(last & has_after)
    def _():
        for k in range(SLAB):
            greet(at(z + 1, k, col))

    @pl.when(first & has_before)
    def _():
        for k in range(SLAB):
            greet(at(z - 1, k, col))

    @pl.when(has_before)
    def _():
        greet(at(z - 1, SLAB - 1, col))

    @pl.when(has_after)
    def _():
        greet(at(z + 1, 0, col))

    def yes(flag):
        return jnp.where(flag, 1, 0)

    expected = (
        slabs - 1 + SLAB - 1 + 1 + (cols - 2) * yes(col == 0)
        + SLAB * yes(last & has_after) + SLAB * yes(first & has_before)
        + yes(has_before) + yes(has_after)
    )

    @pl.when(z == 0)
    def _():
        before0[...] = jnp.zeros_like(before0)
        beforec[...] = jnp.zeros_like(beforec)

    @pl.when(in_tail)
    def _():
        after0[...] = jnp.zeros_like(after0)

    keep_c = pltpu.make_async_copy(x_ref, slabc.at[y], local_sem.at[0])
    keep_c.start()
    pl.semaphore_wait(barrier, expected)

    @pl.when(col == 0)
    def _():
        for k in range(1, cols):
            remote(x_ref.at[0:1, :], own0.at[0:1, :], send_0.at[k], recv_0.at[0], at(z, y, k)).start()
        own = pltpu.make_async_copy(x_ref.at[0:1, :], own0.at[0:1, :], local_sem.at[1])
        own.start()
        own.wait()

    for k in range(1, SLAB):
        remote(x_ref, slabc.at[y], send_x.at[k], recv_x.at[y], at(z, (y + k) % SLAB, col)).start()

    @pl.when(last & has_after)
    def _():
        remote(x_ref.at[:, cut:], beforec, send_hc.at[0], recv_hc.at[0], at(z + 1, 0, col)).start()

    @pl.when(col != 0)
    def _():
        remote(x_ref.at[0:1, :], own0.at[0:1, :], send_0.at[0], recv_0.at[0], at(z, y, 0)).wait_recv()

    keep_0 = pltpu.make_async_copy(own0.at[0:1, :], slab0.at[y, 0:1, :], local_sem.at[2])
    keep_0.start()
    for k in range(1, SLAB):
        remote(
            own0.at[0:1, :], slab0.at[y, 0:1, :], send_s0.at[k], recv_s0.at[y], at(z, (y + k) % SLAB, col)
        ).start()

    @pl.when(last & has_after)
    def _():
        for k in range(SLAB):
            remote(
                own0.at[0:1, cut:], before0.at[0:1, :], send_hb.at[k], recv_hb.at[0], at(z + 1, k, col)
            ).start()

    @pl.when(first & has_before)
    def _():
        for k in range(SLAB):
            remote(
                own0.at[0:1, :TAPS], after0.at[0:1, :], send_ha.at[k], recv_ha.at[0], at(z - 1, k, col)
            ).start()

    keep_c.wait()
    keep_0.wait()
    for k in range(1, SLAB):
        other = (y + k) % SLAB
        remote(x_ref, slabc.at[other], send_x.at[k], recv_x.at[other], at(z, other, col)).wait_recv()
        remote(
            own0.at[0:1, :], slab0.at[other, 0:1, :], send_s0.at[k], recv_s0.at[other], at(z, other, col)
        ).wait_recv()

    @pl.when(has_before)
    def _():
        remote(own0.at[0:1, cut:], before0.at[0:1, :], send_hb.at[0], recv_hb.at[0], at(z, y, col)).wait_recv()

    @pl.when(has_after)
    def _():
        remote(own0.at[0:1, :TAPS], after0.at[0:1, :], send_ha.at[0], recv_ha.at[0], at(z, y, col)).wait_recv()

    def tails(k):
        where = at((z + k) % slabs, y, col)
        return (
            remote(slab0.at[SLAB - 1, 0:1, cut:], tail0.at[0:1, :], send_t.at[0, k], recv_t.at[0], where),
            remote(slabc.at[SLAB - 1, :, cut:], tailc, send_t.at[1, k], recv_t.at[1], where),
        )

    @pl.when(in_tail)
    def _():
        @pl.loop(1, slabs)
        def _(k):
            for copy in tails(k):
                copy.start()

        tail0[0:1, :] = slab0[SLAB - 1, 0:1, cut:]
        tailc[...] = slabc[SLAB - 1, :, cut:]

    per = rows // 128
    count = SLAB * per
    block0 = [before0[0:1, 0:128], before0[0:1, 128:256]]
    for j in range(SLAB):
        block0 += [slab0[j, 0:1, 128 * b : 128 * b + 128] for b in range(per)]
    block0 += [after0[0:1, 0:128], after0[0:1, 128:256]]
    ext0 = jnp.concatenate(block0, axis=0)
    wide0 = jnp.concatenate([ext0[k : k + count] for k in range(5)], axis=1)
    place = iota((count, 640), 0) * 128 + iota((count, 640), 1) - 256
    late = count * 128 - (TAPS - 1)
    wide0_early = jnp.where(in_tail & (place >= late), 0.0, wide0)
    right = jnp.concatenate([wide0, wide0_early[count - 8 :]], axis=0)
    flip = anti_identity()
    at_late = in_tail & (iota((count, 128), 0) * 128 + iota((count, 128), 1) >= late)
    lefts = []
    for t in range(3):
        if t == 0:
            mine = ext0[2 : 2 + count]
        else:
            mine = jnp.concatenate(
                [slabc[j, t - 1 : t, 128 * b : 128 * b + 128] for j in range(SLAB) for b in range(per)], axis=0
            )
        lefts += [jnp.where(at_late, 0.0, mine), jnp.where(at_late, mine, 0.0)[count - 8 :]]
    flipped = dot(jnp.concatenate(lefts, axis=0), flip)
    deep = count + 8
    for t in range(3):
        table = dot(flipped[deep * t : deep * t + deep], right, 0, 0)
        skewed = pltpu.roll(table, 1, 1, stride=1, stride_axis=0)
        summed = jnp.sum(skewed, axis=0, keepdims=True)
        for b in range(4):
            lags[z, 4 * t + b : 4 * t + b + 1, :] = summed[:, 128 + 128 * b : 256 + 128 * b]

    def exchange(k):
        where = at((z + k) % slabs, y, col)
        return remote(lags.at[z], lags.at[z], send_l.at[k], recv_l.at[z], where)

    @pl.loop(1, slabs)
    def _(k):
        exchange(k).start()

    ext_ref[0:1, TAPS:] = own0[0:1, :]
    ext_ref[1:3, TAPS:] = x_ref[...]

    @pl.when(first)
    def _():
        ext_ref[0:1, :TAPS] = before0[0:1, :]

        @pl.when(has_before)
        def _():
            remote(x_ref.at[:, cut:], beforec, send_hc.at[0], recv_hc.at[0], at(z, y, col)).wait_recv()

        ext_ref[1:3, :TAPS] = beforec[...]

    @pl.when(y > 0)
    def _():
        ext_ref[0:1, :TAPS] = slab0[(y + SLAB - 1) % SLAB, 0:1, cut:]
        ext_ref[1:3, :TAPS] = slabc[(y + SLAB - 1) % SLAB, :, cut:]

    @pl.when(z < slabs - 1)
    def _():
        for copy in tails(0):
            copy.wait_recv()

    tail_ref[0:1, :] = tail0[0:1, :]
    tail_ref[1:3, :] = tailc[...]

    @pl.loop(1, slabs)
    def _(k):
        other = (z + k) % slabs
        remote(lags.at[other], lags.at[other], send_l.at[k], recv_l.at[other], at(other, y, col)).wait_recv()

    total = lags[0]
    for k in range(1, slabs):
        total = total + lags[k]
    sums_ref[...] = total

    @pl.when(col == 0)
    def _():
        for k in range(1, cols):
            remote(x_ref.at[0:1, :], own0.at[0:1, :], send_0.at[k], recv_0.at[0], at(z, y, k)).wait_send()

    for k in range(1, SLAB):
        other = (y + k) % SLAB
        remote(x_ref, slabc.at[y], send_x.at[k], recv_x.at[y], at(z, other, col)).wait_send()
        remote(
            own0.at[0:1, :], slab0.at[y, 0:1, :], send_s0.at[k], recv_s0.at[y], at(z, other, col)
        ).wait_send()

    @pl.when(last & has_after)
    def _():
        remote(x_ref.at[:, cut:], beforec, send_hc.at[0], recv_hc.at[0], at(z + 1, 0, col)).wait_send()
        for k in range(SLAB):
            remote(
                own0.at[0:1, cut:], before0.at[0:1, :], send_hb.at[k], recv_hb.at[0], at(z + 1, k, col)
            ).wait_send()

    @pl.when(first & has_before)
    def _():
        for k in range(SLAB):
            remote(
                own0.at[0:1, :TAPS], after0.at[0:1, :], send_ha.at[k], recv_ha.at[0], at(z - 1, k, col)
            ).wait_send()

    @pl.when(in_tail)
    def _():
        @pl.loop(1, slabs)
        def _(k):
            for copy in tails(k):
                copy.wait_send()

    @pl.loop(1, slabs)
    def _(k):
        exchange(k).wait_send()


def lag_sums(traces, slabs, cols):
    rows = traces.shape[1]
    f32, dma = jnp.float32, pltpu.SemaphoreType.DMA
    return pl.pallas_call(
        functools.partial(lag_kernel, slabs, cols),
        name="lag_sums",
        out_shape=(
            jax.ShapeDtypeStruct((12, 128), f32),
            jax.ShapeDtypeStruct((3, rows + TAPS), f32),
            jax.ShapeDtypeStruct((3, TAPS), f32),
        ),
        in_specs=[VM],
        out_specs=(VM, VM, VM),
        scratch_shapes=[
            pltpu.VMEM((2, rows), f32),
            pltpu.VMEM((SLAB, 2, rows), f32),
            pltpu.VMEM((SLAB, 2, rows), f32),
            pltpu.VMEM((2, TAPS), f32),
            pltpu.VMEM((2, TAPS), f32),
            pltpu.VMEM((2, TAPS), f32),
            pltpu.VMEM((2, TAPS), f32),
            pltpu.VMEM((2, TAPS), f32),
            pltpu.VMEM((slabs, 12, 128), f32),
            dma((3,)),
            dma((SLAB,)), dma((SLAB,)),
            dma((cols,)), dma((1,)),
            dma((1,)), dma((1,)),
            dma((SLAB,)), dma((SLAB,)),
            dma((SLAB,)), dma((1,)),
            dma((SLAB,)), dma((1,)),
            dma((2, slabs)), dma((2,)),
            dma((slabs,)), dma((slabs,)),
        ],
        compiler_params=pltpu.CompilerParams(collective_id=0, has_side_effects=True),
    )(traces)


def factor_inverse(work, size):
    sub = iota((8, 128), 0)
    lane = iota((8, size), 1)
    for k in range(size // 8):
        here = work[8 * k : 8 * k + 8, :]
        cols = [jnp.broadcast_to(here[:, 8 * k + j : 8 * k + j + 1], (8, 128)) for j in range(8)]
        invs = [jnp.where(sub == j, 1.0, 0.0).astype(jnp.float32) for j in range(8)]
        for j in range(8):
            scale = lax.rsqrt(jnp.broadcast_to(cols[j][j : j + 1], (8, 128)))
            below = jnp.where(sub > j, cols[j] * scale, 0.0)
            for m in range(j + 1, 8):
                cols[m] = cols[m] - below * (jnp.broadcast_to(cols[m][j : j + 1], (8, 128)) * scale)
            for m in range(j + 1):
                piv = jnp.broadcast_to(invs[m][j : j + 1], (8, 128)) * scale
                invs[m] = jnp.where(sub == j, piv, invs[m] - below * piv)
        done = None
        for m in range(8):
            wide = jnp.concatenate([invs[m]] * (2 * size // 128), axis=1) * jnp.broadcast_to(here[m : m + 1, :], (8, 2 * size))
            done = wide if done is None else done + wide
        work[8 * k : 8 * k + 8, :] = done
        if 8 * k + 8 < size:
            left = jnp.where(lane > 8 * k + 7, done[:, :size], 0.0)
            change = dot(left, done, 0, 0)
            work[8 * k + 8 :, :] = work[8 * k + 8 :, :] - change[8 * k + 8 :, :]


def remainder_kernel(count, sums_ref, ext_ref, tail_ref, over_ref, coup_ref, work, low):
    flip = anti_identity()
    blocks = (ext_ref.shape[1]) // 128
    ext = jnp.concatenate(
        [ext_ref[t : t + 1, 128 * b : 128 * b + 128] for t in range(3) for b in range(blocks)], axis=0
    )
    flipped = dot(ext, flip)

    def toeplitz(t):
        row = jnp.concatenate(
            [flipped[blocks * t + b : blocks * t + b + 1] for b in reversed(range(blocks))], axis=1
        )
        turned = pltpu.roll(jnp.broadcast_to(row, (128, 128 * blocks)), 1, 1, stride=1, stride_axis=0)
        return jnp.concatenate(
            [
                jnp.concatenate([turned[:, 512 - 128 * (s - k) :][:, :128] for k in range(2)], axis=1)
                for s in range(blocks - 2)
            ],
            axis=0,
        )

    zero = jnp.zeros((128, 128), jnp.float32)

    def late(t):
        tail = jnp.where(iota((1, TAPS), 1) == 0, 0.0, tail_ref[t : t + 1, :])
        row = jnp.concatenate([jnp.zeros((1, 128), jnp.float32), tail], axis=1)
        turned = pltpu.roll(jnp.broadcast_to(row, (128, 384)), 0, 1, stride=1, stride_axis=0)
        top = jnp.concatenate([turned[:, 128:256], turned[:, 256:384]], axis=1)
        return jnp.concatenate([top, jnp.concatenate([zero, turned[:, 128:256]], axis=1)], axis=0)

    def early(t):
        row = jnp.concatenate([sums_ref[4 * t + b : 4 * t + b + 1, :] for b in range(4)], axis=1)
        turned = pltpu.roll(jnp.broadcast_to(row, (128, 512)), 0, 1, stride=1, stride_axis=0)
        return jnp.concatenate(
            [
                jnp.concatenate([turned[:, 256 + 128 * (k - s) :][:, :128] for k in range(2)], axis=1)
                for s in range(2)
            ],
            axis=0,
        )

    late0 = late(0)
    gram = (early(0) + dot(late0, late0, 1, 1)) / count
    eye = jnp.where(iota((128, 128), 0) == iota((128, 128), 1), 1.0, 0.0).astype(jnp.float32)
    work[:, :128] = gram[:128, :128]
    work[:, 128:] = eye
    factor_inverse(work, 128)
    first = work[:, 128:]
    below = dot(gram[128:, :128], first, 1, 1)
    work[:, :128] = gram[128:, 128:] - dot(below, below, 1, 1)
    work[:, 128:] = eye
    factor_inverse(work, 128)
    second = work[:, 128:]
    low[:128, :128] = first
    low[:128, 128:] = zero
    low[128:, :128] = -dot(second, dot(below, first))
    low[128:, 128:] = second
    inverse = low[...]

    basis = dot(toeplitz(0), inverse, 1, 1)
    for t in range(2):
        cross = (early(1 + t) + dot(late0, late(1 + t), 1, 1)) / count
        coupled = dot(inverse, cross)
        coup_ref[:, 256 * t : 256 * t + 256] = coupled
        over_ref[:, 256 * t : 256 * t + 256] = toeplitz(1 + t) - dot(basis, coupled)

    @pl.when(lax.axis_index("col") == 0)
    def _():
        over_ref[:, :WIDE] = basis


def remainder(sums, ext, tail, count):
    rows = ext.shape[1] - TAPS
    f32 = jnp.float32
    return pl.pallas_call(
        functools.partial(remainder_kernel, count),
        name="remainder",
        out_shape=(jax.ShapeDtypeStruct((rows, 512), f32), jax.ShapeDtypeStruct((WIDE, 512), f32)),
        in_specs=[VM, VM, VM],
        out_specs=(VM, VM),
        scratch_shapes=[pltpu.VMEM((128, 256), f32), pltpu.VMEM((256, 256), f32)],
    )(sums, ext, tail)


def solution(mesh):
    slabs, cols = mesh.shape["row"] // SLAB, mesh.shape["col"]

    def body(traces):
        count = traces.shape[1] * slabs * SLAB
        sums, ext, tail = lag_sums(traces, slabs, cols)
        return remainder(sums, ext, tail, count)

    return jax.shard_map(
        body,
        mesh=mesh,
        in_specs=(P("col", "row"),),
        out_specs=(P("row", "col"), P(None, "col")),
        check_vma=False,
    )
```

```python
import functools

import jax
import jax.numpy as jnp
from jax import lax
from jax.experimental import pallas as pl
from jax.experimental.pallas import tpu as pltpu
from jax.sharding import PartitionSpec as P

TAPS = 256
WIDE = 256
SLAB = 4
MESH = pl.DeviceIdType.MESH
HIGHEST = lax.Precision.HIGHEST
VM = pl.BlockSpec(memory_space=pltpu.VMEM)


def dot(a, b, da=1, db=0):
    return lax.dot_general(
        a, b, (((da,), (db,)), ((), ())), precision=HIGHEST, preferred_element_type=jnp.float32
    )


def iota(shape, axis):
    return lax.broadcasted_iota(jnp.int32, shape, axis)


def anti_identity():
    return jnp.where(iota((128, 128), 0) + iota((128, 128), 1) == 127, 1.0, 0.0).astype(jnp.float32)


def lag_kernel(
    slabs, cols,
    x_ref, sums_ref, ext_ref, tail_ref,
    own0, slab0, slabc, before0, after0, beforec, tail0, tailc, lags,
    local_sem, send_x, recv_x, send_0, recv_0, send_hc, recv_hc,
    send_s0, recv_s0, send_hb, recv_hb, send_ha, recv_ha, send_t, recv_t, send_l, recv_l,
):
    row, col = lax.axis_index("row"), lax.axis_index("col")
    z, y = row // SLAB, row % SLAB
    rows = x_ref.shape[1]
    cut = rows - TAPS
    first, last = y == 0, y == SLAB - 1
    has_before, has_after = z > 0, z < slabs - 1
    in_tail = z == slabs - 1

    def at(zz, yy, cc):
        return (zz * SLAB + yy, cc)

    def remote(src, dst, send, recv, where):
        return pltpu.make_async_remote_copy(
            src_ref=src, dst_ref=dst, send_sem=send, recv_sem=recv, device_id=where, device_id_type=MESH
        )

    barrier = pltpu.get_barrier_semaphore()

    def greet(where):
        pl.semaphore_signal(barrier, inc=1, device_id=where, device_id_type=MESH)

    @pl.loop(1, slabs)
    def _(k):
        greet(at((z + k) % slabs, y, col))

    for k in range(1, SLAB):
        greet(at(z, (y + k) % SLAB, col))

    @pl.when(col == 0)
    def _():
        for k in range(1, cols):
            greet(at(z, y, k))

    @pl.when(col != 0)
    def _():
        greet(at(z, y, 0))

    @pl.when(last & has_after)
    def _():
        for k in range(SLAB):
            greet(at(z + 1, k, col))

    @pl.when(first & has_before)
    def _():
        for k in range(SLAB):
            greet(at(z - 1, k, col))

    @pl.when(has_before)
    def _():
        greet(at(z - 1, SLAB - 1, col))

    @pl.when(has_after)
    def _():
        greet(at(z + 1, 0, col))

    def yes(flag):
        return jnp.where(flag, 1, 0)

    expected = (
        slabs - 1 + SLAB - 1 + 1 + (cols - 2) * yes(col == 0)
        + SLAB * yes(last & has_after) + SLAB * yes(first & has_before)
        + yes(has_before) + yes(has_after)
    )

    @pl.when(z == 0)
    def _():
        before0[...] = jnp.zeros_like(before0)
        beforec[...] = jnp.zeros_like(beforec)

    @pl.when(in_tail)
    def _():
        after0[...] = jnp.zeros_like(after0)

    keep_c = pltpu.make_async_copy(x_ref, slabc.at[y], local_sem.at[0])
    keep_c.start()
    pl.semaphore_wait(barrier, expected)

    @pl.when(col == 0)
    def _():
        for k in range(1, cols):
            remote(x_ref.at[0:1, :], own0.at[0:1, :], send_0.at[k], recv_0.at[0], at(z, y, k)).start()
        own = pltpu.make_async_copy(x_ref.at[0:1, :], own0.at[0:1, :], local_sem.at[1])
        own.start()
        own.wait()

    for k in range(1, SLAB):
        remote(x_ref, slabc.at[y], send_x.at[k], recv_x.at[y], at(z, (y + k) % SLAB, col)).start()

    @pl.when(last & has_after)
    def _():
        remote(x_ref.at[:, cut:], beforec, send_hc.at[0], recv_hc.at[0], at(z + 1, 0, col)).start()

    @pl.when(col != 0)
    def _():
        remote(x_ref.at[0:1, :], own0.at[0:1, :], send_0.at[0], recv_0.at[0], at(z, y, 0)).wait_recv()

    keep_0 = pltpu.make_async_copy(own0.at[0:1, :], slab0.at[y, 0:1, :], local_sem.at[2])
    keep_0.start()
    for k in range(1, SLAB):
        remote(
            own0.at[0:1, :], slab0.at[y, 0:1, :], send_s0.at[k], recv_s0.at[y], at(z, (y + k) % SLAB, col)
        ).start()

    @pl.when(last & has_after)
    def _():
        for k in range(SLAB):
            remote(
                own0.at[0:1, cut:], before0.at[0:1, :], send_hb.at[k], recv_hb.at[0], at(z + 1, k, col)
            ).start()

    @pl.when(first & has_before)
    def _():
        for k in range(SLAB):
            remote(
                own0.at[0:1, :TAPS], after0.at[0:1, :], send_ha.at[k], recv_ha.at[0], at(z - 1, k, col)
            ).start()

    keep_c.wait()
    keep_0.wait()
    for k in range(1, SLAB):
        other = (y + k) % SLAB
        remote(x_ref, slabc.at[other], send_x.at[k], recv_x.at[other], at(z, other, col)).wait_recv()
        remote(
            own0.at[0:1, :], slab0.at[other, 0:1, :], send_s0.at[k], recv_s0.at[other], at(z, other, col)
        ).wait_recv()

    @pl.when(has_before)
    def _():
        remote(own0.at[0:1, cut:], before0.at[0:1, :], send_hb.at[0], recv_hb.at[0], at(z, y, col)).wait_recv()

    @pl.when(has_after)
    def _():
        remote(own0.at[0:1, :TAPS], after0.at[0:1, :], send_ha.at[0], recv_ha.at[0], at(z, y, col)).wait_recv()

    def tails(k):
        where = at((z + k) % slabs, y, col)
        return (
            remote(slab0.at[SLAB - 1, 0:1, cut:], tail0.at[0:1, :], send_t.at[0, k], recv_t.at[0], where),
            remote(slabc.at[SLAB - 1, :, cut:], tailc, send_t.at[1, k], recv_t.at[1], where),
        )

    @pl.when(in_tail)
    def _():
        @pl.loop(1, slabs)
        def _(k):
            for copy in tails(k):
                copy.start()

        tail0[0:1, :] = slab0[SLAB - 1, 0:1, cut:]
        tailc[...] = slabc[SLAB - 1, :, cut:]

    per = rows // 128
    count = SLAB * per
    block0 = [before0[0:1, 0:128], before0[0:1, 128:256]]
    for j in range(SLAB):
        block0 += [slab0[j, 0:1, 128 * b : 128 * b + 128] for b in range(per)]
    block0 += [after0[0:1, 0:128], after0[0:1, 128:256]]
    ext0 = jnp.concatenate(block0, axis=0)
    wide0 = jnp.concatenate([ext0[k : k + count] for k in range(5)], axis=1)
    place = iota((count, 640), 0) * 128 + iota((count, 640), 1) - 256
    late = count * 128 - (TAPS - 1)
    wide0_early = jnp.where(in_tail & (place >= late), 0.0, wide0)
    right = jnp.concatenate([wide0, wide0_early[count - 8 :]], axis=0)
    flip = anti_identity()
    at_late = in_tail & (iota((count, 128), 0) * 128 + iota((count, 128), 1) >= late)
    lefts = []
    for t in range(3):
        if t == 0:
            mine = ext0[2 : 2 + count]
        else:
            mine = jnp.concatenate(
                [slabc[j, t - 1 : t, 128 * b : 128 * b + 128] for j in range(SLAB) for b in range(per)], axis=0
            )
        lefts += [jnp.where(at_late, 0.0, mine), jnp.where(at_late, mine, 0.0)[count - 8 :]]
    flipped = dot(jnp.concatenate(lefts, axis=0), flip)
    deep = count + 8
    for t in range(3):
        table = dot(flipped[deep * t : deep * t + deep], right, 0, 0)
        skewed = pltpu.roll(table, 1, 1, stride=1, stride_axis=0)
        summed = jnp.sum(skewed, axis=0, keepdims=True)
        for b in range(4):
            lags[z, 4 * t + b : 4 * t + b + 1, :] = summed[:, 128 + 128 * b : 256 + 128 * b]

    def exchange(k):
        where = at((z + k) % slabs, y, col)
        return remote(lags.at[z], lags.at[z], send_l.at[k], recv_l.at[z], where)

    @pl.loop(1, slabs)
    def _(k):
        exchange(k).start()

    ext_ref[0:1, TAPS:] = own0[0:1, :]
    ext_ref[1:3, TAPS:] = x_ref[...]

    @pl.when(first)
    def _():
        ext_ref[0:1, :TAPS] = before0[0:1, :]

        @pl.when(has_before)
        def _():
            remote(x_ref.at[:, cut:], beforec, send_hc.at[0], recv_hc.at[0], at(z, y, col)).wait_recv()

        ext_ref[1:3, :TAPS] = beforec[...]

    @pl.when(y > 0)
    def _():
        ext_ref[0:1, :TAPS] = slab0[(y + SLAB - 1) % SLAB, 0:1, cut:]
        ext_ref[1:3, :TAPS] = slabc[(y + SLAB - 1) % SLAB, :, cut:]

    @pl.when(z < slabs - 1)
    def _():
        for copy in tails(0):
            copy.wait_recv()

    tail_ref[0:1, :] = tail0[0:1, :]
    tail_ref[1:3, :] = tailc[...]

    @pl.loop(1, slabs)
    def _(k):
        other = (z + k) % slabs
        remote(lags.at[other], lags.at[other], send_l.at[k], recv_l.at[other], at(other, y, col)).wait_recv()

    total = lags[0]
    for k in range(1, slabs):
        total = total + lags[k]
    sums_ref[...] = total

    @pl.when(col == 0)
    def _():
        for k in range(1, cols):
            remote(x_ref.at[0:1, :], own0.at[0:1, :], send_0.at[k], recv_0.at[0], at(z, y, k)).wait_send()

    for k in range(1, SLAB):
        other = (y + k) % SLAB
        remote(x_ref, slabc.at[y], send_x.at[k], recv_x.at[y], at(z, other, col)).wait_send()
        remote(
            own0.at[0:1, :], slab0.at[y, 0:1, :], send_s0.at[k], recv_s0.at[y], at(z, other, col)
        ).wait_send()

    @pl.when(last & has_after)
    def _():
        remote(x_ref.at[:, cut:], beforec, send_hc.at[0], recv_hc.at[0], at(z + 1, 0, col)).wait_send()
        for k in range(SLAB):
            remote(
                own0.at[0:1, cut:], before0.at[0:1, :], send_hb.at[k], recv_hb.at[0], at(z + 1, k, col)
            ).wait_send()

    @pl.when(first & has_before)
    def _():
        for k in range(SLAB):
            remote(
                own0.at[0:1, :TAPS], after0.at[0:1, :], send_ha.at[k], recv_ha.at[0], at(z - 1, k, col)
            ).wait_send()

    @pl.when(in_tail)
    def _():
        @pl.loop(1, slabs)
        def _(k):
            for copy in tails(k):
                copy.wait_send()

    @pl.loop(1, slabs)
    def _(k):
        exchange(k).wait_send()


def lag_sums(traces, slabs, cols):
    rows = traces.shape[1]
    f32, dma = jnp.float32, pltpu.SemaphoreType.DMA
    return pl.pallas_call(
        functools.partial(lag_kernel, slabs, cols),
        name="lag_sums",
        out_shape=(
            jax.ShapeDtypeStruct((12, 128), f32),
            jax.ShapeDtypeStruct((3, rows + TAPS), f32),
            jax.ShapeDtypeStruct((3, TAPS), f32),
        ),
        in_specs=[VM],
        out_specs=(VM, VM, VM),
        scratch_shapes=[
            pltpu.VMEM((2, rows), f32),
            pltpu.VMEM((SLAB, 2, rows), f32),
            pltpu.VMEM((SLAB, 2, rows), f32),
            pltpu.VMEM((2, TAPS), f32),
            pltpu.VMEM((2, TAPS), f32),
            pltpu.VMEM((2, TAPS), f32),
            pltpu.VMEM((2, TAPS), f32),
            pltpu.VMEM((2, TAPS), f32),
            pltpu.VMEM((slabs, 12, 128), f32),
            dma((3,)),
            dma((SLAB,)), dma((SLAB,)),
            dma((cols,)), dma((1,)),
            dma((1,)), dma((1,)),
            dma((SLAB,)), dma((SLAB,)),
            dma((SLAB,)), dma((1,)),
            dma((SLAB,)), dma((1,)),
            dma((2, slabs)), dma((2,)),
            dma((slabs,)), dma((slabs,)),
        ],
        compiler_params=pltpu.CompilerParams(
            collective_id=0, has_side_effects=True, vmem_limit_bytes=8 * 2**20
        ),
    )(traces)


def split(x):
    high = x.astype(jnp.bfloat16)
    return high, (x - high.astype(jnp.float32)).astype(jnp.bfloat16)


def dot3(a, b, nt=False):
    (ah, al), (bh, bl) = a, b
    left = jnp.concatenate([ah, al, ah], axis=1)
    right = jnp.concatenate([bh, bh, bl], axis=1 if nt else 0)
    return lax.dot_general(
        left, right, (((1,), (1 if nt else 0,)), ((), ())), preferred_element_type=jnp.float32
    )


def tree(terms):
    while len(terms) > 1:
        terms = [terms[i] + terms[i + 1] if i + 1 < len(terms) else terms[i] for i in range(0, len(terms), 2)]
    return terms[0]


def pick(v, j):
    return jnp.broadcast_to(v[j : j + 1], (8, 128))


def eliminate(cols):
    sub = iota((8, 128), 0)
    cols = list(cols)
    invs = [jnp.where(sub == j, 1.0, 0.0).astype(jnp.float32) for j in range(8)]
    scales = None
    for j in range(8):
        scale = lax.rsqrt(pick(cols[j], j))
        scales = scale if scales is None else jnp.where(sub == j, scale, scales)
        if j == 7:
            break
        below = jnp.where(sub > j, cols[j], 0.0)
        square = scale * scale
        ratio = below * square
        cols[j + 1] = cols[j + 1] - (below * pick(cols[j + 1], j)) * square
        for m in range(j + 2, 8):
            cols[m] = cols[m] - ratio * pick(cols[m], j)
        for m in range(j):
            invs[m] = invs[m] - ratio * pick(invs[m], j)
        invs[j] = invs[j] - ratio
    return [v * scales for v in invs]


def thirds(x):
    high = x.astype(jnp.bfloat16).astype(jnp.float32)
    rest = x - high
    mid = rest.astype(jnp.bfloat16).astype(jnp.float32)
    return high, mid, rest - mid


def outer6(a, b):
    (ah, am, al), (bh, bm, bl) = a, b
    left = jnp.concatenate([ah, ah, am, am, ah, al], axis=0).astype(jnp.bfloat16)
    right = jnp.concatenate([bh, bm, bh, bm, bl, bh], axis=0).astype(jnp.bfloat16)
    return lax.dot_general(left, right, (((0,), (0,)), ((), ())), preferred_element_type=jnp.float32)


def factor_inverse(blocks, beside):
    count = len(blocks)
    beside = list(beside)
    due = [i * (count - 1) // len(beside) for i in range(len(beside))]
    mat = list(blocks)
    lane, sub = iota((8, 128), 1), iota((8, 128), 0)
    out = [jnp.where(lane == sub + 8 * i, 1.0, 0.0).astype(jnp.float32) for i in range(count)]

    def column(i, c):
        return jnp.broadcast_to(mat[i][:, c : c + 1], (8, 128))

    def apply(vectors, block):
        return tree([vectors[m] * pick(block, m) for m in range(8)])

    cols = [column(0, m) for m in range(8)]
    for k in range(count):
        invs = eliminate(cols)
        out[k] = apply(invs, out[k])
        if k + 1 == count:
            break
        done = apply(invs, mat[k])
        nxt = k + 1
        by = [column(nxt, 8 * k + m) for m in range(8)]
        factor = [tree([by[m] * pick(invs[m], j) for m in range(j + 1)]) for j in range(8)]
        if True:
            old = [column(nxt, 8 * nxt + m) for m in range(8)]
            cols = [old[m] - tree([factor[j] * pick(factor[j], m) for j in range(8)]) for m in range(8)]
        mat[nxt] = mat[nxt] - apply(factor, done)
        out[nxt] = out[nxt] - apply(factor, out[k])
        if not True:
            cols = [column(nxt, 8 * nxt + m) for m in range(8)]
        if nxt + 1 < count:
            both = thirds(jnp.concatenate([done, out[k]], axis=1))
            change = outer6([part[:, :128] for part in both], both)
            for i in range(nxt + 1, count):
                mat[i] = mat[i] - change[8 * i : 8 * i + 8, :128]
                out[i] = out[i] - change[8 * i : 8 * i + 8, 128:]
        for when, piece in zip(due, beside):
            if when == k:
                piece()
    return out


def dot6(a, b):
    (ah, am, al), (bh, bm, bl) = ([v.astype(jnp.bfloat16) for v in x] for x in (a, b))

    def part(u, v):
        return lax.dot_general(u, v, (((1,), (1,)), ((), ())), preferred_element_type=jnp.float32)

    def beside(u, v):
        return jnp.concatenate([u, v], axis=1)

    size = bh.shape[0]
    main = part(beside(ah, am), jnp.concatenate([beside(bh, bm), beside(bm, bh)], axis=0))
    return main[:, :size] + (main[:, size:] + part(beside(ah, al), beside(bl, bh)))


def remainder_kernel(
    count, sums_ref, ext_ref, tail_ref, over_ref, coup_ref, panel_ref, panel2_ref, basis_ref, cross_ref, flip_ref
):
    blocks = (ext_ref.shape[1]) // 128
    steps = blocks - 2
    parts = 128 * steps // 512

    def late(t):
        tail = jnp.where(iota((1, TAPS), 1) == 0, 0.0, tail_ref[t : t + 1, :])
        row = jnp.concatenate([jnp.zeros((1, 128), jnp.float32), tail], axis=1)
        turned = pltpu.roll(jnp.broadcast_to(row, (128, 384)), 0, 1, stride=1, stride_axis=0)
        return turned[:, 128:256], turned[:, 256:384]

    def early(t):
        row = jnp.concatenate([sums_ref[4 * t + b : 4 * t + b + 1, :] for b in range(4)], axis=1)
        turned = pltpu.roll(jnp.broadcast_to(row, (128, 512)), 0, 1, stride=1, stride_axis=0)
        return turned[:, 256:512], turned[:, 128:384]

    near0, far0 = late(0)
    gram_top, gram_low = early(0)
    near6, far6 = thirds(near0), thirds(far0)
    near_near = dot6(near6, near6)
    gram11 = (gram_top[:, :128] + (near_near + dot6(far6, far6))) / count
    got = {}

    def gram_rest():
        got["gram21"] = thirds((gram_low[:, :128] + dot6(near6, far6)) / count)
        got["gram22"] = (gram_low[:, 128:] + near_near) / count

    def turn_around():
        ext = jnp.concatenate(
            [ext_ref[t : t + 1, 128 * b : 128 * b + 128] for t in range(3) for b in range(blocks)], axis=0
        )
        flip_ref[0 : 3 * blocks, :] = dot(ext, anti_identity())

    def toeplitz(t):
        def piece():
            row = jnp.concatenate(
                [flip_ref[blocks * t + b : blocks * t + b + 1, :] for b in reversed(range(blocks))], axis=1
            )
            turned = pltpu.roll(jnp.broadcast_to(row, (128, 128 * blocks)), 1, 1, stride=1, stride_axis=0)
            for k in range(2):
                for s in range(steps):
                    rows, at = slice(128 * s, 128 * s + 128), 128 * k
                    block = turned[:, 512 + 128 * (k - s) : 640 + 128 * (k - s)]
                    if t == 0:
                        panel_ref[rows, at : at + 128] = block
                    else:
                        over_ref[rows, 256 * (t - 1) + at : 256 * (t - 1) + at + 128] = block

        return piece

    def cross(t):
        def piece():
            near, far = late(t)
            top, low = early(t)
            near_a, far_a, near_c, far_c = split(near0), split(far0), split(near), split(far)
            same = dot3(near_a, near_c, True)
            at = 256 * (t - 1)
            cross_ref[:128, at : at + 128] = (top[:, :128] + (same + dot3(far_a, far_c, True))) / count
            cross_ref[:128, at + 128 : at + 256] = (top[:, 128:] + dot3(far_a, near_c, True)) / count
            cross_ref[128:, at : at + 128] = (low[:, :128] + dot3(near_a, far_c, True)) / count
            cross_ref[128:, at + 128 : at + 256] = (low[:, 128:] + same) / count

        return piece

    first = jnp.concatenate(
        factor_inverse(
            [gram11[8 * i : 8 * i + 8] for i in range(16)],
            [gram_rest, turn_around] + [toeplitz(t) for t in range(3)] + [cross(1 + t) for t in range(2)],
        ),
        axis=0,
    )
    below = dot6(got["gram21"], thirds(first))
    below6 = thirds(below)
    schur = got["gram22"] - dot6(below6, below6)
    first2, below2 = split(first), split(below)

    def wide(i):
        return slice(256 * i, 256 * i + 256)

    def couple(i):
        def piece():
            coup_ref[:128, wide(i)] = dot3(first2, split(cross_ref[:128, wide(i)]))

        return piece

    def couple_rest(i):
        def piece():
            cross_ref[128:, wide(i)] = cross_ref[128:, wide(i)] - dot3(below2, split(coup_ref[:128, wide(i)]))

        return piece

    def upper(s):
        return slice(512 * s, 512 * s + 512)

    def orthogonalize(s):
        def piece():
            basis_ref[upper(s), :] = dot3(split(panel_ref[upper(s), :128]), first2, True)

        return piece

    def orthogonalize_rest(s):
        def piece():
            panel2_ref[upper(s), :] = panel_ref[upper(s), 128:] - dot3(split(basis_ref[upper(s), :]), below2, True)

        return piece

    def project(s, i):
        def piece():
            change = dot3(split(basis_ref[upper(s), :]), split(coup_ref[:128, wide(i)]))
            over_ref[upper(s), wide(i)] = over_ref[upper(s), wide(i)] - change

        return piece

    second = jnp.concatenate(
        factor_inverse(
            [schur[8 * i : 8 * i + 8] for i in range(16)],
            [couple(i) for i in range(2)]
            + [orthogonalize(s) for s in range(parts)]
            + [project(s, i) for i in range(2) for s in range(parts)]
            + [couple_rest(i) for i in range(2)]
            + [orthogonalize_rest(s) for s in range(parts)],
        ),
        axis=0,
    )
    second2 = split(second)
    basis2 = dot3(split(panel2_ref[...]), second2, True)
    panel2_ref[...] = basis2
    basis2s = split(basis2)
    for i in range(2):
        coup2 = dot3(second2, split(cross_ref[128:, wide(i)]))
        coup_ref[128:, wide(i)] = coup2
        over_ref[:, wide(i)] = over_ref[:, wide(i)] - dot3(basis2s, split(coup2))

    @pl.when(lax.axis_index("col") == 0)
    def _():
        over_ref[:, :128] = basis_ref[...]
        over_ref[:, 128:WIDE] = panel2_ref[...]


def remainder(sums, ext, tail, count):
    rows = ext.shape[1] - TAPS
    f32 = jnp.float32
    return pl.pallas_call(
        functools.partial(remainder_kernel, count),
        name="remainder",
        out_shape=(jax.ShapeDtypeStruct((rows, 512), f32), jax.ShapeDtypeStruct((WIDE, 512), f32)),
        in_specs=[VM, VM, VM],
        out_specs=(VM, VM),
        scratch_shapes=[
            pltpu.VMEM((rows, WIDE), f32),
            pltpu.VMEM((rows, 128), f32),
            pltpu.VMEM((rows, 128), f32),
            pltpu.VMEM((WIDE, 512), f32),
            pltpu.VMEM((24, 128), f32),
        ],
        compiler_params=pltpu.CompilerParams(vmem_limit_bytes=24 * 2**20),
    )(sums, ext, tail)


def solution(mesh):
    slabs, cols = mesh.shape["row"] // SLAB, mesh.shape["col"]

    def body(traces):
        count = traces.shape[1] * slabs * SLAB
        sums, ext, tail = lag_sums(traces, slabs, cols)
        return remainder(sums, ext, tail, count)

    return jax.shard_map(
        body,
        mesh=mesh,
        in_specs=(P("col", "row"),),
        out_specs=(P("row", "col"), P(None, "col")),
        check_vma=False,
    )
```

```python
import functools

import jax
import jax.numpy as jnp
from jax import lax
from jax.experimental import pallas as pl
from jax.experimental.pallas import tpu as pltpu
from jax.sharding import PartitionSpec as P

TAPS = 256
WIDE = 256
SLAB = 4
MESH = pl.DeviceIdType.MESH
HIGHEST = lax.Precision.HIGHEST
VM = pl.BlockSpec(memory_space=pltpu.VMEM)


def dot(a, b, da=1, db=0):
    return lax.dot_general(
        a, b, (((da,), (db,)), ((), ())), precision=HIGHEST, preferred_element_type=jnp.float32
    )


def iota(shape, axis):
    return lax.broadcasted_iota(jnp.int32, shape, axis)


def anti_identity():
    return jnp.where(iota((128, 128), 0) + iota((128, 128), 1) == 127, 1.0, 0.0).astype(jnp.float32)


def lag_kernel(
    slabs, cols,
    x_ref, sums_ref, ext_ref, tail_ref,
    mine, own0, slab0, slabc, before0, after0, beforec, late0, latec, lags,
    local_sem, send_x, recv_x, send_0, recv_0, send_hc, recv_hc,
    send_s0, recv_s0, send_hb, recv_hb, send_ha, recv_ha, send_t, recv_t, send_l, recv_l, hello,
):
    row, col = lax.axis_index("row"), lax.axis_index("col")
    z, y = row // SLAB, row % SLAB
    per = x_ref.shape[1] // 128
    first, last = y == 0, y == SLAB - 1
    has_before, has_after = z > 0, z < slabs - 1
    in_tail = z == slabs - 1

    def at(zz, yy, cc):
        return (zz * SLAB + yy, cc)

    def around(k):
        return at((z + k + slabs) % slabs, y, col)

    def remote(src, dst, send, recv, where):
        return pltpu.make_async_remote_copy(
            src_ref=src, dst_ref=dst, send_sem=send, recv_sem=recv, device_id=where, device_id_type=MESH
        )

    barrier = pltpu.get_barrier_semaphore()

    def greet(where):
        pl.semaphore_signal(barrier, inc=1, device_id=where, device_id_type=MESH)

    greet(around(1))
    greet(around(-1))

    @pl.when(last & has_after)
    def _():
        for k in range(SLAB):
            greet(at(z + 1, k, col))

    @pl.when(first & has_before)
    def _():
        for k in range(SLAB):
            greet(at(z - 1, k, col))

    @pl.when(has_before)
    def _():
        greet(at(z - 1, SLAB - 1, col))

    @pl.when(has_after)
    def _():
        greet(at(z + 1, 0, col))

    @pl.when(col == 0)
    def _():
        for k in range(1, cols):
            greet(at(z, y, k))

    @pl.when(col != 0)
    def _():
        greet(at(z, y, 0))

    for k in range(1, SLAB):
        greet(at(z, (y + k) % SLAB, col))

    def yes(flag):
        return jnp.where(flag, 1, 0)

    expected = (
        2 + SLAB - 1 + yes(col != 0) + (cols - 1) * yes(col == 0)
        + SLAB * yes(last & has_after) + SLAB * yes(first & has_before)
        + yes(has_before) + yes(has_after)
    )

    @pl.when(z == 0)
    def _():
        before0[...] = jnp.zeros_like(before0)
        beforec[...] = jnp.zeros_like(beforec)

    @pl.when(in_tail)
    def _():
        after0[...] = jnp.zeros_like(after0)

    plain = jnp.concatenate(
        [x_ref[t : t + 1, 128 * b : 128 * b + 128] for t in range(2) for b in range(per)], axis=0
    )
    turned = dot(plain, anti_identity())
    mine[...] = turned
    slabc[y] = turned

    @pl.when(col == 0)
    def _():
        own0[:per, :] = plain[:per]
        own0[per:, :] = turned[:per]

    pl.semaphore_wait(barrier, expected)

    @pl.when(col == 0)
    def _():
        for k in range(1, cols):
            remote(own0, own0, send_0.at[k], recv_0.at[0], at(z, y, k)).start()

    for k in range(1, SLAB):
        remote(mine, slabc.at[y], send_x.at[k], recv_x.at[y], at(z, (y + k) % SLAB, col)).start()

    @pl.when(last & has_after)
    def _():
        remote(mine, beforec, send_hc.at[0], recv_hc.at[0], at(z + 1, 0, col)).start()

    reach = [r for r in (1, 2, 4, 8, 16) if 4 * r <= slabs]

    def tell(i):
        for k in (reach[i], -reach[i]):
            pl.semaphore_signal(hello.at[i], inc=1, device_id=around(k), device_id_type=MESH)

    if reach:
        tell(0)
    if len(reach) > 1:
        pl.semaphore_wait(hello.at[0], 2)
        tell(1)

    @pl.when(col != 0)
    def _():
        remote(own0, own0, send_0.at[0], recv_0.at[0], at(z, y, 0)).wait_recv()

    keep_0 = pltpu.make_async_copy(own0, slab0.at[y], local_sem.at[0])
    keep_0.start()
    for k in range(1, SLAB):
        remote(own0, slab0.at[y], send_s0.at[k], recv_s0.at[y], at(z, (y + k) % SLAB, col)).start()

    @pl.when(last & has_after)
    def _():
        for k in range(SLAB):
            remote(own0, before0, send_hb.at[k], recv_hb.at[0], at(z + 1, k, col)).start()

    @pl.when(first & has_before)
    def _():
        for k in range(SLAB):
            remote(own0.at[0:2], after0, send_ha.at[k], recv_ha.at[0], at(z - 1, k, col)).start()

    for i in range(2, len(reach)):
        pl.semaphore_wait(hello.at[i - 1], 2)
        tell(i)

    keep_0.wait()
    for k in range(1, SLAB):
        other = (y + k) % SLAB
        remote(mine, slabc.at[other], send_x.at[k], recv_x.at[other], at(z, other, col)).wait_recv()
        remote(own0, slab0.at[other], send_s0.at[k], recv_s0.at[other], at(z, other, col)).wait_recv()

    @pl.when(has_before)
    def _():
        remote(own0, before0, send_hb.at[0], recv_hb.at[0], at(z, y, col)).wait_recv()

    @pl.when(has_after)
    def _():
        remote(own0.at[0:2], after0, send_ha.at[0], recv_ha.at[0], at(z, y, col)).wait_recv()

    count = SLAB * per
    ext0 = jnp.concatenate([before0[per - 2 : per, :]] + [slab0[j, :per, :] for j in range(SLAB)] + [after0[...]], axis=0)
    wide0 = jnp.concatenate([ext0[k : k + count] for k in range(5)], axis=1)
    place = iota((count, 640), 0) * 128 + iota((count, 640), 1) - 256
    late = count * 128 - (TAPS - 1)
    wide0_early = jnp.where(in_tail & (place >= late), 0.0, wide0)
    right = jnp.concatenate([wide0, wide0_early[count - 8 :]], axis=0)
    at_late = in_tail & (iota((count, 128), 0) * 128 + 127 - iota((count, 128), 1) >= late)
    lefts = []
    for t in range(3):
        if t == 0:
            group = jnp.concatenate([slab0[j, per:, :] for j in range(SLAB)], axis=0)
        else:
            group = jnp.concatenate([slabc[j, per * (t - 1) : per * t, :] for j in range(SLAB)], axis=0)
        lefts.append(
            jnp.concatenate([jnp.where(at_late, 0.0, group), jnp.where(at_late, group, 0.0)[count - 8 :]], axis=0)
        )
    table = outer6(thirds(jnp.concatenate(lefts, axis=1)), thirds(right))
    for t in range(3):
        skewed = pltpu.roll(table[128 * t : 128 * t + 128], 1, 1, stride=1, stride_axis=0)
        summed = jnp.sum(skewed, axis=0, keepdims=True)
        for b in range(4):
            lags[z, 4 * t + b : 4 * t + b + 1, :] = summed[:, 128 + 128 * b : 256 + 128 * b]

    if reach:
        pl.semaphore_wait(hello.at[len(reach) - 1], 2)

    def exchange(k):
        return remote(lags.at[z], lags.at[z], send_l.at[k], recv_l.at[z], around(k))

    @pl.loop(0, slabs - 1)
    def _(k):
        exchange(1 + (k + slabs // 2 - 1) % (slabs - 1)).start()

    def tails(k):
        return (
            remote(slab0.at[SLAB - 1, per - 2 : per], late0, send_t.at[0, k], recv_t.at[0], around(k)),
            remote(slabc.at[SLAB - 1, per - 2 : per], latec.at[0], send_t.at[1, k], recv_t.at[1], around(k)),
            remote(slabc.at[SLAB - 1, 2 * per - 2 :], latec.at[1], send_t.at[2, k], recv_t.at[2], around(k)),
        )

    @pl.when(in_tail)
    def _():
        @pl.loop(1, slabs)
        def _(k):
            for copy in tails(k):
                copy.start()

        late0[...] = slab0[SLAB - 1, per - 2 : per]
        latec[0] = slabc[SLAB - 1, per - 2 : per]
        latec[1] = slabc[SLAB - 1, 2 * per - 2 :]

    reach_back = per + 2
    ext_ref[2:reach_back, :] = own0[per:, :]
    for t in range(2):
        ext_ref[reach_back * (t + 1) + 2 : reach_back * (t + 2), :] = mine[per * t : per * t + per, :]

    @pl.when(first)
    def _():
        @pl.when(has_before)
        def _():
            remote(mine, beforec, send_hc.at[0], recv_hc.at[0], at(z, y, col)).wait_recv()

        ext_ref[0:2, :] = before0[2 * per - 2 :, :]
        for t in range(2):
            ext_ref[reach_back * (t + 1) : reach_back * (t + 1) + 2, :] = beforec[per * t + per - 2 : per * t + per, :]

    @pl.when(y > 0)
    def _():
        before = (y + SLAB - 1) % SLAB
        ext_ref[0:2, :] = slab0[before, 2 * per - 2 :, :]
        for t in range(2):
            ext_ref[reach_back * (t + 1) : reach_back * (t + 1) + 2, :] = slabc[before, per * t + per - 2 : per * t + per, :]

    @pl.when(z < slabs - 1)
    def _():
        for copy in tails(0):
            copy.wait_recv()

    tail_ref[0:2, :] = late0[...]
    tail_ref[2:4, :] = latec[0]
    tail_ref[4:6, :] = latec[1]
    tail_ref[6:8, :] = jnp.zeros((2, 128), jnp.float32)

    @pl.loop(1, slabs)
    def _(k):
        other = (z + k) % slabs
        remote(lags.at[other], lags.at[other], send_l.at[k], recv_l.at[other], at(other, y, col)).wait_recv()

    sums_ref[...] = tree([lags[k] for k in range(slabs)])

    @pl.when(col == 0)
    def _():
        for k in range(1, cols):
            remote(own0, own0, send_0.at[k], recv_0.at[0], at(z, y, k)).wait_send()

    for k in range(1, SLAB):
        other = (y + k) % SLAB
        remote(mine, slabc.at[y], send_x.at[k], recv_x.at[y], at(z, other, col)).wait_send()
        remote(own0, slab0.at[y], send_s0.at[k], recv_s0.at[y], at(z, other, col)).wait_send()

    @pl.when(last & has_after)
    def _():
        remote(mine, beforec, send_hc.at[0], recv_hc.at[0], at(z + 1, 0, col)).wait_send()
        for k in range(SLAB):
            remote(own0, before0, send_hb.at[k], recv_hb.at[0], at(z + 1, k, col)).wait_send()

    @pl.when(first & has_before)
    def _():
        for k in range(SLAB):
            remote(own0.at[0:2], after0, send_ha.at[k], recv_ha.at[0], at(z - 1, k, col)).wait_send()

    @pl.when(in_tail)
    def _():
        @pl.loop(1, slabs)
        def _(k):
            for copy in tails(k):
                copy.wait_send()

    @pl.loop(1, slabs)
    def _(k):
        exchange(k).wait_send()


def lag_sums(traces, slabs, cols):
    per = traces.shape[1] // 128
    f32, dma = jnp.float32, pltpu.SemaphoreType.DMA
    return pl.pallas_call(
        functools.partial(lag_kernel, slabs, cols),
        name="lag_sums",
        out_shape=(
            jax.ShapeDtypeStruct((12, 128), f32),
            jax.ShapeDtypeStruct((3 * (per + 2), 128), f32),
            jax.ShapeDtypeStruct((8, 128), f32),
        ),
        in_specs=[VM],
        out_specs=(VM, VM, VM),
        scratch_shapes=[
            pltpu.VMEM((2 * per, 128), f32),
            pltpu.VMEM((2 * per, 128), f32),
            pltpu.VMEM((SLAB, 2 * per, 128), f32),
            pltpu.VMEM((SLAB, 2 * per, 128), f32),
            pltpu.VMEM((2 * per, 128), f32),
            pltpu.VMEM((2, 128), f32),
            pltpu.VMEM((2 * per, 128), f32),
            pltpu.VMEM((2, 128), f32),
            pltpu.VMEM((2, 2, 128), f32),
            pltpu.VMEM((slabs, 12, 128), f32),
            dma((1,)),
            dma((SLAB,)), dma((SLAB,)),
            dma((cols,)), dma((1,)),
            dma((1,)), dma((1,)),
            dma((SLAB,)), dma((SLAB,)),
            dma((SLAB,)), dma((1,)),
            dma((SLAB,)), dma((1,)),
            dma((3, slabs)), dma((3,)),
            dma((slabs,)), dma((slabs,)),
            pltpu.SemaphoreType.REGULAR((5,)),
        ],
        compiler_params=pltpu.CompilerParams(
            collective_id=0, has_side_effects=True, vmem_limit_bytes=8 * 2**20
        ),
    )(traces)


def split(x):
    high = x.astype(jnp.bfloat16)
    return high, (x - high.astype(jnp.float32)).astype(jnp.bfloat16)


def dot3(a, b, nt=False):
    (ah, al), (bh, bl) = a, b
    left = jnp.concatenate([ah, al, ah], axis=1)
    right = jnp.concatenate([bh, bh, bl], axis=1 if nt else 0)
    return lax.dot_general(
        left, right, (((1,), (1 if nt else 0,)), ((), ())), preferred_element_type=jnp.float32
    )


def tree(terms):
    while len(terms) > 1:
        terms = [terms[i] + terms[i + 1] if i + 1 < len(terms) else terms[i] for i in range(0, len(terms), 2)]
    return terms[0]


def pick(v, j):
    return jnp.broadcast_to(v[j : j + 1], (8, 128))


def eliminate(cols):
    sub = iota((8, 128), 0)
    cols = list(cols)
    invs = [jnp.where(sub == j, 1.0, 0.0).astype(jnp.float32) for j in range(8)]
    scales = None
    for j in range(8):
        scale = lax.rsqrt(pick(cols[j], j))
        scales = scale if scales is None else jnp.where(sub == j, scale, scales)
        if j == 7:
            break
        below = jnp.where(sub > j, cols[j], 0.0)
        square = scale * scale
        ratio = below * square
        cols[j + 1] = cols[j + 1] - (below * pick(cols[j + 1], j)) * square
        for m in range(j + 2, 8):
            cols[m] = cols[m] - ratio * pick(cols[m], j)
        for m in range(j):
            invs[m] = invs[m] - ratio * pick(invs[m], j)
        invs[j] = invs[j] - ratio
    return [v * scales for v in invs]


def thirds(x):
    high = x.astype(jnp.bfloat16).astype(jnp.float32)
    rest = x - high
    mid = rest.astype(jnp.bfloat16).astype(jnp.float32)
    return high, mid, rest - mid


def outer6(a, b):
    (ah, am, al), (bh, bm, bl) = a, b
    left = jnp.concatenate([ah, ah, am, am, ah, al], axis=0).astype(jnp.bfloat16)
    right = jnp.concatenate([bh, bm, bh, bm, bl, bh], axis=0).astype(jnp.bfloat16)
    return lax.dot_general(left, right, (((0,), (0,)), ((), ())), preferred_element_type=jnp.float32)


def factor_inverse(blocks, beside):
    count = len(blocks)
    beside = list(beside)
    due = [i * (count - 1) // len(beside) for i in range(len(beside))]
    mat = list(blocks)
    lane, sub = iota((8, 128), 1), iota((8, 128), 0)
    out = [jnp.where(lane == sub + 8 * i, 1.0, 0.0).astype(jnp.float32) for i in range(count)]

    def column(i, c):
        return jnp.broadcast_to(mat[i][:, c : c + 1], (8, 128))

    def apply(vectors, block):
        return tree([vectors[m] * pick(block, m) for m in range(8)])

    cols = [column(0, m) for m in range(8)]
    for k in range(count):
        invs = eliminate(cols)
        out[k] = apply(invs, out[k])
        if k + 1 == count:
            break
        done = apply(invs, mat[k])
        nxt = k + 1
        by = [column(nxt, 8 * k + m) for m in range(8)]
        factor = [tree([by[m] * pick(invs[m], j) for m in range(j + 1)]) for j in range(8)]
        if True:
            old = [column(nxt, 8 * nxt + m) for m in range(8)]
            cols = [old[m] - tree([factor[j] * pick(factor[j], m) for j in range(8)]) for m in range(8)]
        mat[nxt] = mat[nxt] - apply(factor, done)
        out[nxt] = out[nxt] - apply(factor, out[k])
        if not True:
            cols = [column(nxt, 8 * nxt + m) for m in range(8)]
        if nxt + 1 < count:
            both = thirds(jnp.concatenate([done, out[k]], axis=1))
            change = outer6([part[:, :128] for part in both], both)
            for i in range(nxt + 1, count):
                mat[i] = mat[i] - change[8 * i : 8 * i + 8, :128]
                out[i] = out[i] - change[8 * i : 8 * i + 8, 128:]
        for when, piece in zip(due, beside):
            if when == k:
                piece()
    return out


def dot6(a, b):
    (ah, am, al), (bh, bm, bl) = ([v.astype(jnp.bfloat16) for v in x] for x in (a, b))

    def part(u, v):
        return lax.dot_general(u, v, (((1,), (1,)), ((), ())), preferred_element_type=jnp.float32)

    def beside(u, v):
        return jnp.concatenate([u, v], axis=1)

    size = bh.shape[0]
    main = part(beside(ah, am), jnp.concatenate([beside(bh, bm), beside(bm, bh)], axis=0))
    return main[:, :size] + (main[:, size:] + part(beside(ah, al), beside(bl, bh)))


def remainder_kernel(
    count, sums_ref, ext_ref, tail_ref, over_ref, coup_ref, panel_ref, panel2_ref, basis_ref, cross_ref
):
    blocks = ext_ref.shape[0] // 3
    steps = blocks - 2
    parts = 128 * steps // 512

    def late(t):
        rows = tail_ref[0:2, :] if t == 0 else dot(tail_ref[...], anti_identity())[2 * t : 2 * t + 2]
        tail = jnp.where(iota((1, TAPS), 1) == 0, 0.0, jnp.concatenate([rows[0:1], rows[1:2]], axis=1))
        row = jnp.concatenate([jnp.zeros((1, 128), jnp.float32), tail], axis=1)
        turned = pltpu.roll(jnp.broadcast_to(row, (128, 384)), 0, 1, stride=1, stride_axis=0)
        return turned[:, 128:256], turned[:, 256:384]

    def early(t):
        row = jnp.concatenate([sums_ref[4 * t + b : 4 * t + b + 1, :] for b in range(4)], axis=1)
        turned = pltpu.roll(jnp.broadcast_to(row, (128, 512)), 0, 1, stride=1, stride_axis=0)
        return turned[:, 256:512], turned[:, 128:384]

    near0, far0 = late(0)
    gram_top, gram_low = early(0)
    near6, far6 = thirds(near0), thirds(far0)
    near_near = dot6(near6, near6)
    gram11 = (gram_top[:, :128] + (near_near + dot6(far6, far6))) / count
    got = {}

    def gram_rest():
        got["gram21"] = thirds((gram_low[:, :128] + dot6(near6, far6)) / count)
        got["gram22"] = (gram_low[:, 128:] + near_near) / count

    def toeplitz(t):
        def piece():
            row = jnp.concatenate(
                [ext_ref[blocks * t + b : blocks * t + b + 1, :] for b in reversed(range(blocks))], axis=1
            )
            turned = pltpu.roll(jnp.broadcast_to(row, (128, 128 * blocks)), 1, 1, stride=1, stride_axis=0)
            for k in range(2):
                for s in range(steps):
                    rows, at = slice(128 * s, 128 * s + 128), 128 * k
                    block = turned[:, 512 + 128 * (k - s) : 640 + 128 * (k - s)]
                    if t == 0:
                        panel_ref[rows, at : at + 128] = block
                    else:
                        over_ref[rows, 256 * (t - 1) + at : 256 * (t - 1) + at + 128] = block

        return piece

    def cross(t):
        def piece():
            near, far = late(t)
            top, low = early(t)
            near_a, far_a, near_c, far_c = split(near0), split(far0), split(near), split(far)
            same = dot3(near_a, near_c, True)
            at = 256 * (t - 1)
            cross_ref[:128, at : at + 128] = (top[:, :128] + (same + dot3(far_a, far_c, True))) / count
            cross_ref[:128, at + 128 : at + 256] = (top[:, 128:] + dot3(far_a, near_c, True)) / count
            cross_ref[128:, at : at + 128] = (low[:, :128] + dot3(near_a, far_c, True)) / count
            cross_ref[128:, at + 128 : at + 256] = (low[:, 128:] + same) / count

        return piece

    first = jnp.concatenate(
        factor_inverse(
            [gram11[8 * i : 8 * i + 8] for i in range(16)],
            [gram_rest] + [toeplitz(t) for t in range(3)] + [cross(1 + t) for t in range(2)],
        ),
        axis=0,
    )
    below = dot6(got["gram21"], thirds(first))
    below6 = thirds(below)
    schur = got["gram22"] - dot6(below6, below6)
    first2, below2 = split(first), split(below)

    def wide(i):
        return slice(256 * i, 256 * i + 256)

    def couple(i):
        def piece():
            coup_ref[:128, wide(i)] = dot3(first2, split(cross_ref[:128, wide(i)]))

        return piece

    def couple_rest(i):
        def piece():
            cross_ref[128:, wide(i)] = cross_ref[128:, wide(i)] - dot3(below2, split(coup_ref[:128, wide(i)]))

        return piece

    def upper(s):
        return slice(512 * s, 512 * s + 512)

    def orthogonalize(s):
        def piece():
            basis_ref[upper(s), :] = dot3(split(panel_ref[upper(s), :128]), first2, True)

        return piece

    def orthogonalize_rest(s):
        def piece():
            panel2_ref[upper(s), :] = panel_ref[upper(s), 128:] - dot3(split(basis_ref[upper(s), :]), below2, True)

        return piece

    def project(s, i):
        def piece():
            change = dot3(split(basis_ref[upper(s), :]), split(coup_ref[:128, wide(i)]))
            over_ref[upper(s), wide(i)] = over_ref[upper(s), wide(i)] - change

        return piece

    second = jnp.concatenate(
        factor_inverse(
            [schur[8 * i : 8 * i + 8] for i in range(16)],
            [couple(i) for i in range(2)]
            + [orthogonalize(s) for s in range(parts)]
            + [project(s, i) for i in range(2) for s in range(parts)]
            + [couple_rest(i) for i in range(2)]
            + [orthogonalize_rest(s) for s in range(parts)],
        ),
        axis=0,
    )
    second2 = split(second)
    basis2 = dot3(split(panel2_ref[...]), second2, True)
    panel2_ref[...] = basis2
    basis2s = split(basis2)
    for i in range(2):
        coup2 = dot3(second2, split(cross_ref[128:, wide(i)]))
        coup_ref[128:, wide(i)] = coup2
        over_ref[:, wide(i)] = over_ref[:, wide(i)] - dot3(basis2s, split(coup2))

    @pl.when(lax.axis_index("col") == 0)
    def _():
        over_ref[:, :128] = basis_ref[...]
        over_ref[:, 128:WIDE] = panel2_ref[...]


def remainder(sums, ext, tail, count):
    rows = 128 * (ext.shape[0] // 3) - TAPS
    f32 = jnp.float32
    return pl.pallas_call(
        functools.partial(remainder_kernel, count),
        name="remainder",
        out_shape=(jax.ShapeDtypeStruct((rows, 512), f32), jax.ShapeDtypeStruct((WIDE, 512), f32)),
        in_specs=[VM, VM, VM],
        out_specs=(VM, VM),
        scratch_shapes=[
            pltpu.VMEM((rows, WIDE), f32),
            pltpu.VMEM((rows, 128), f32),
            pltpu.VMEM((rows, 128), f32),
            pltpu.VMEM((WIDE, 512), f32),
        ],
        compiler_params=pltpu.CompilerParams(vmem_limit_bytes=24 * 2**20),
    )(sums, ext, tail)


def solution(mesh):
    slabs, cols = mesh.shape["row"] // SLAB, mesh.shape["col"]

    def body(traces):
        count = traces.shape[1] * slabs * SLAB
        sums, ext, tail = lag_sums(traces, slabs, cols)
        return remainder(sums, ext, tail, count)

    return jax.shard_map(
        body,
        mesh=mesh,
        in_specs=(P("col", "row"),),
        out_specs=(P("row", "col"), P(None, "col")),
        check_vma=False,
    )
```

```python
import functools

import jax
import jax.numpy as jnp
from jax import lax
from jax.experimental import pallas as pl
from jax.experimental.pallas import tpu as pltpu
from jax.sharding import PartitionSpec as P

TAPS = 256
WIDE = 256
SLAB = 4
MESH = pl.DeviceIdType.MESH
HIGHEST = lax.Precision.HIGHEST
VM = pl.BlockSpec(memory_space=pltpu.VMEM)


def dot(a, b, da=1, db=0):
    return lax.dot_general(
        a, b, (((da,), (db,)), ((), ())), precision=HIGHEST, preferred_element_type=jnp.float32
    )


def iota(shape, axis):
    return lax.broadcasted_iota(jnp.int32, shape, axis)


def anti_identity():
    return jnp.where(iota((128, 128), 0) + iota((128, 128), 1) == 127, 1.0, 0.0).astype(jnp.float32)


def lag_kernel(
    slabs, cols,
    x_hbm, sums_ref, late_ref, panel_ref, block_ref,
    x_ref, ext_ref, mine, own0, slab0, slabc, before0, after0, beforec, late0, latec, lags,
    local_sem, send_x, recv_x, send_0, recv_0, send_hc, recv_hc,
    send_s0, recv_s0, send_hb, recv_hb, send_ha, recv_ha, send_t, recv_t, send_l, recv_l, hello,
):
    fetch = pltpu.make_async_copy(x_hbm, x_ref, local_sem.at[1])
    fetch.start()
    row, col = lax.axis_index("row"), lax.axis_index("col")
    z, y = row // SLAB, row % SLAB
    per = x_ref.shape[1] // 128
    first, last = y == 0, y == SLAB - 1
    has_before, has_after = z > 0, z < slabs - 1
    in_tail = z == slabs - 1

    def at(zz, yy, cc):
        return (zz * SLAB + yy, cc)

    def around(k):
        return at((z + k + slabs) % slabs, y, col)

    def remote(src, dst, send, recv, where):
        return pltpu.make_async_remote_copy(
            src_ref=src, dst_ref=dst, send_sem=send, recv_sem=recv, device_id=where, device_id_type=MESH
        )

    barrier = pltpu.get_barrier_semaphore()

    def greet(where):
        pl.semaphore_signal(barrier, inc=1, device_id=where, device_id_type=MESH)

    greet(around(1))
    greet(around(-1))

    @pl.when(last & has_after)
    def _():
        for k in range(SLAB):
            greet(at(z + 1, k, col))

    @pl.when(first & has_before)
    def _():
        for k in range(SLAB):
            greet(at(z - 1, k, col))

    @pl.when(has_before)
    def _():
        greet(at(z - 1, SLAB - 1, col))

    @pl.when(has_after)
    def _():
        greet(at(z + 1, 0, col))

    @pl.when(col == 0)
    def _():
        for k in range(1, cols):
            greet(at(z, y, k))

    @pl.when(col != 0)
    def _():
        greet(at(z, y, 0))

    for k in range(1, SLAB):
        greet(at(z, (y + k) % SLAB, col))

    def yes(flag):
        return jnp.where(flag, 1, 0)

    expected = (
        2 + SLAB - 1 + yes(col != 0) + (cols - 1) * yes(col == 0)
        + SLAB * yes(last & has_after) + SLAB * yes(first & has_before)
        + yes(has_before) + yes(has_after)
    )

    @pl.when(z == 0)
    def _():
        before0[...] = jnp.zeros_like(before0)
        beforec[...] = jnp.zeros_like(beforec)

    @pl.when(in_tail)
    def _():
        after0[...] = jnp.zeros_like(after0)

    fetch.wait()
    plain = jnp.concatenate(
        [x_ref[t : t + 1, 128 * b : 128 * b + 128] for t in range(2) for b in range(per)], axis=0
    )
    turned = dot(plain, anti_identity())
    mine[...] = turned
    slabc[y] = turned

    @pl.when(col == 0)
    def _():
        own0[:per, :] = plain[:per]
        own0[per:, :] = turned[:per]

    pl.semaphore_wait(barrier, expected)

    @pl.when(col == 0)
    def _():
        for k in range(1, cols):
            remote(own0, own0, send_0.at[k], recv_0.at[0], at(z, y, k)).start()

    for k in range(1, SLAB):
        remote(mine, slabc.at[y], send_x.at[k], recv_x.at[y], at(z, (y + k) % SLAB, col)).start()

    @pl.when(last & has_after)
    def _():
        remote(mine, beforec, send_hc.at[0], recv_hc.at[0], at(z + 1, 0, col)).start()

    reach = [r for r in (1, 2, 4, 8, 16) if 4 * r <= slabs]

    def tell(i):
        for k in (reach[i], -reach[i]):
            pl.semaphore_signal(hello.at[i], inc=1, device_id=around(k), device_id_type=MESH)

    if reach:
        tell(0)
    if len(reach) > 1:
        pl.semaphore_wait(hello.at[0], 2)
        tell(1)

    @pl.when(col != 0)
    def _():
        remote(own0, own0, send_0.at[0], recv_0.at[0], at(z, y, 0)).wait_recv()

    keep_0 = pltpu.make_async_copy(own0, slab0.at[y], local_sem.at[0])
    keep_0.start()
    for k in range(1, SLAB):
        remote(own0, slab0.at[y], send_s0.at[k], recv_s0.at[y], at(z, (y + k) % SLAB, col)).start()

    @pl.when(last & has_after)
    def _():
        for k in range(SLAB):
            remote(own0, before0, send_hb.at[k], recv_hb.at[0], at(z + 1, k, col)).start()

    @pl.when(first & has_before)
    def _():
        for k in range(SLAB):
            remote(own0.at[0:2], after0, send_ha.at[k], recv_ha.at[0], at(z - 1, k, col)).start()

    for i in range(2, len(reach)):
        pl.semaphore_wait(hello.at[i - 1], 2)
        tell(i)

    keep_0.wait()
    for k in range(1, SLAB):
        other = (y + k) % SLAB
        remote(mine, slabc.at[other], send_x.at[k], recv_x.at[other], at(z, other, col)).wait_recv()
        remote(own0, slab0.at[other], send_s0.at[k], recv_s0.at[other], at(z, other, col)).wait_recv()

    @pl.when(has_before)
    def _():
        remote(own0, before0, send_hb.at[0], recv_hb.at[0], at(z, y, col)).wait_recv()

    @pl.when(has_after)
    def _():
        remote(own0.at[0:2], after0, send_ha.at[0], recv_ha.at[0], at(z, y, col)).wait_recv()

    def all_came():
        if reach:
            pl.semaphore_wait(hello.at[len(reach) - 1], 2)

    def tails(k):
        return (
            remote(slab0.at[SLAB - 1, per - 2 : per], late0, send_t.at[0, k], recv_t.at[0], around(k)),
            remote(slabc.at[SLAB - 1, per - 2 : per], latec.at[0], send_t.at[1, k], recv_t.at[1], around(k)),
            remote(slabc.at[SLAB - 1, 2 * per - 2 :], latec.at[1], send_t.at[2, k], recv_t.at[2], around(k)),
        )

    @pl.when(in_tail)
    def _():
        all_came()

        @pl.loop(1, slabs)
        def _(k):
            for copy in tails(k):
                copy.start()

        late0[...] = slab0[SLAB - 1, per - 2 : per]
        latec[0] = slabc[SLAB - 1, per - 2 : per]
        latec[1] = slabc[SLAB - 1, 2 * per - 2 :]

    count = SLAB * per
    ext0 = jnp.concatenate([before0[per - 2 : per, :]] + [slab0[j, :per, :] for j in range(SLAB)] + [after0[...]], axis=0)
    wide0 = jnp.concatenate([ext0[k : k + count] for k in range(5)], axis=1)
    place = iota((count, 640), 0) * 128 + iota((count, 640), 1) - 256
    late = count * 128 - (TAPS - 1)
    wide0_early = jnp.where(in_tail & (place >= late), 0.0, wide0)
    right = jnp.concatenate([wide0, wide0_early[count - 8 :]], axis=0)
    at_late = in_tail & (iota((count, 128), 0) * 128 + 127 - iota((count, 128), 1) >= late)
    lefts = []
    for t in range(3):
        if t == 0:
            group = jnp.concatenate([slab0[j, per:, :] for j in range(SLAB)], axis=0)
        else:
            group = jnp.concatenate([slabc[j, per * (t - 1) : per * t, :] for j in range(SLAB)], axis=0)
        lefts.append(
            jnp.concatenate([jnp.where(at_late, 0.0, group), jnp.where(at_late, group, 0.0)[count - 8 :]], axis=0)
        )
    table = outer6(thirds(jnp.concatenate(lefts, axis=1)), thirds(right))
    for t in range(3):
        skewed = pltpu.roll(table[128 * t : 128 * t + 128], 1, 1, stride=1, stride_axis=0)
        summed = jnp.sum(skewed, axis=0, keepdims=True)
        for b in range(4):
            lags[z, 4 * t + b : 4 * t + b + 1, :] = summed[:, 128 + 128 * b : 256 + 128 * b]

    def exchange(k):
        return remote(lags.at[z], lags.at[z], send_l.at[k], recv_l.at[z], around(k))

    pl.when(z < slabs - 1)(all_came)

    @pl.loop(0, slabs - 1)
    def _(k):
        exchange(1 + (k + slabs // 2 - 1) % (slabs - 1)).start()

    reach_back = per + 2
    ext_ref[2:reach_back, :] = own0[per:, :]
    for t in range(2):
        ext_ref[reach_back * (t + 1) + 2 : reach_back * (t + 2), :] = mine[per * t : per * t + per, :]

    @pl.when(first)
    def _():
        @pl.when(has_before)
        def _():
            remote(mine, beforec, send_hc.at[0], recv_hc.at[0], at(z, y, col)).wait_recv()

        ext_ref[0:2, :] = before0[2 * per - 2 :, :]
        for t in range(2):
            ext_ref[reach_back * (t + 1) : reach_back * (t + 1) + 2, :] = beforec[per * t + per - 2 : per * t + per, :]

    @pl.when(y > 0)
    def _():
        before = (y + SLAB - 1) % SLAB
        ext_ref[0:2, :] = slab0[before, 2 * per - 2 :, :]
        for t in range(2):
            ext_ref[reach_back * (t + 1) : reach_back * (t + 1) + 2, :] = slabc[before, per * t + per - 2 : per * t + per, :]

    for t in range(3):
        line = jnp.concatenate(
            [ext_ref[reach_back * t + b : reach_back * t + b + 1, :] for b in reversed(range(reach_back))], axis=1
        )
        spun = pltpu.roll(jnp.broadcast_to(line, (128, 128 * reach_back)), 1, 1, stride=1, stride_axis=0)
        for k in range(2):
            for s in range(per):
                block = spun[:, 512 + 128 * (k - s) : 640 + 128 * (k - s)]
                if t == 0:
                    panel_ref[128 * s : 128 * s + 128, 128 * k : 128 * k + 128] = block
                else:
                    block_ref[128 * s : 128 * s + 128, 256 * (t - 1) + 128 * k : 256 * (t - 1) + 128 * k + 128] = block

    @pl.when(z < slabs - 1)
    def _():
        for copy in tails(0):
            copy.wait_recv()

    ends = jnp.concatenate([latec[0], latec[1], jnp.zeros((4, 128), jnp.float32)], axis=0)
    forward = dot(ends, anti_identity())

    def late_rows(t):
        rows = late0[...] if t == 0 else forward[2 * t - 2 : 2 * t]
        tail = jnp.where(iota((1, TAPS), 1) == 0, 0.0, jnp.concatenate([rows[0:1], rows[1:2]], axis=1))
        line = jnp.concatenate([jnp.zeros((1, 128), jnp.float32), tail], axis=1)
        spun = pltpu.roll(jnp.broadcast_to(line, (128, 384)), 0, 1, stride=1, stride_axis=0)
        return spun[:, 128:256], spun[:, 256:384]

    near0, far0 = late_rows(0)
    near6, far6 = thirds(near0), thirds(far0)
    near_near = dot6(near6, near6)
    late_ref[:128, :128] = near_near + dot6(far6, far6)
    late_ref[128:, :128] = dot6(near6, far6)
    late_ref[128:, 128:256] = near_near
    near_a, far_a = split(near0), split(far0)
    for t in (1, 2):
        near_c, far_c = (split(v) for v in late_rows(t))
        same = dot3(near_a, near_c, True)
        late_ref[:128, 256 * t : 256 * t + 128] = same + dot3(far_a, far_c, True)
        late_ref[:128, 256 * t + 128 : 256 * t + 256] = dot3(far_a, near_c, True)
        late_ref[128:, 256 * t : 256 * t + 128] = dot3(near_a, far_c, True)
        late_ref[128:, 256 * t + 128 : 256 * t + 256] = same

    @pl.loop(1, slabs)
    def _(k):
        other = (z + k) % slabs
        remote(lags.at[other], lags.at[other], send_l.at[k], recv_l.at[other], at(other, y, col)).wait_recv()

    sums_ref[...] = tree([lags[k] for k in range(slabs)])

    @pl.when(col == 0)
    def _():
        for k in range(1, cols):
            remote(own0, own0, send_0.at[k], recv_0.at[0], at(z, y, k)).wait_send()

    for k in range(1, SLAB):
        other = (y + k) % SLAB
        remote(mine, slabc.at[y], send_x.at[k], recv_x.at[y], at(z, other, col)).wait_send()
        remote(own0, slab0.at[y], send_s0.at[k], recv_s0.at[y], at(z, other, col)).wait_send()

    @pl.when(last & has_after)
    def _():
        remote(mine, beforec, send_hc.at[0], recv_hc.at[0], at(z + 1, 0, col)).wait_send()
        for k in range(SLAB):
            remote(own0, before0, send_hb.at[k], recv_hb.at[0], at(z + 1, k, col)).wait_send()

    @pl.when(first & has_before)
    def _():
        for k in range(SLAB):
            remote(own0.at[0:2], after0, send_ha.at[k], recv_ha.at[0], at(z - 1, k, col)).wait_send()

    @pl.when(in_tail)
    def _():
        @pl.loop(1, slabs)
        def _(k):
            for copy in tails(k):
                copy.wait_send()

    @pl.loop(1, slabs)
    def _(k):
        exchange(k).wait_send()


def lag_sums(traces, slabs, cols):
    rows = traces.shape[1]
    per = rows // 128
    f32, dma = jnp.float32, pltpu.SemaphoreType.DMA
    return pl.pallas_call(
        functools.partial(lag_kernel, slabs, cols),
        name="lag_sums",
        out_shape=(
            jax.ShapeDtypeStruct((12, 128), f32),
            jax.ShapeDtypeStruct((WIDE, WIDE + 2 * TAPS), f32),
            jax.ShapeDtypeStruct((rows, WIDE), f32),
            jax.ShapeDtypeStruct((rows, 2 * TAPS), f32),
        ),
        in_specs=[pl.BlockSpec(memory_space=pltpu.HBM)],
        out_specs=(VM, VM, VM, VM),
        scratch_shapes=[
            pltpu.VMEM((2, rows), f32),
            pltpu.VMEM((3 * (per + 2), 128), f32),
            pltpu.VMEM((2 * per, 128), f32),
            pltpu.VMEM((2 * per, 128), f32),
            pltpu.VMEM((SLAB, 2 * per, 128), f32),
            pltpu.VMEM((SLAB, 2 * per, 128), f32),
            pltpu.VMEM((2 * per, 128), f32),
            pltpu.VMEM((2, 128), f32),
            pltpu.VMEM((2 * per, 128), f32),
            pltpu.VMEM((2, 128), f32),
            pltpu.VMEM((2, 2, 128), f32),
            pltpu.VMEM((slabs, 12, 128), f32),
            dma((2,)),
            dma((SLAB,)), dma((SLAB,)),
            dma((cols,)), dma((1,)),
            dma((1,)), dma((1,)),
            dma((SLAB,)), dma((SLAB,)),
            dma((SLAB,)), dma((1,)),
            dma((SLAB,)), dma((1,)),
            dma((3, slabs)), dma((3,)),
            dma((slabs,)), dma((slabs,)),
            pltpu.SemaphoreType.REGULAR((5,)),
        ],
        compiler_params=pltpu.CompilerParams(
            collective_id=0, has_side_effects=True, vmem_limit_bytes=12 * 2**20
        ),
    )(traces)


def split(x):
    high = x.astype(jnp.bfloat16)
    return high, (x - high.astype(jnp.float32)).astype(jnp.bfloat16)


def dot3(a, b, nt=False):
    (ah, al), (bh, bl) = a, b
    left = jnp.concatenate([ah, al, ah], axis=1)
    right = jnp.concatenate([bh, bh, bl], axis=1 if nt else 0)
    return lax.dot_general(
        left, right, (((1,), (1 if nt else 0,)), ((), ())), preferred_element_type=jnp.float32
    )


def tree(terms):
    while len(terms) > 1:
        terms = [terms[i] + terms[i + 1] if i + 1 < len(terms) else terms[i] for i in range(0, len(terms), 2)]
    return terms[0]


def pick(v, j):
    return jnp.broadcast_to(v[j : j + 1], (8, 128))


def eliminate(cols):
    sub = iota((8, 128), 0)
    cols = list(cols)
    invs = [jnp.where(sub == j, 1.0, 0.0).astype(jnp.float32) for j in range(8)]
    scales = None
    for j in range(8):
        scale = lax.rsqrt(pick(cols[j], j))
        scales = scale if scales is None else jnp.where(sub == j, scale, scales)
        if j == 7:
            break
        below = jnp.where(sub > j, cols[j], 0.0)
        square = scale * scale
        ratio = below * square
        cols[j + 1] = cols[j + 1] - (below * pick(cols[j + 1], j)) * square
        for m in range(j + 2, 8):
            cols[m] = cols[m] - ratio * pick(cols[m], j)
        for m in range(j):
            invs[m] = invs[m] - ratio * pick(invs[m], j)
        invs[j] = invs[j] - ratio
    return [v * scales for v in invs]


def thirds(x):
    high = x.astype(jnp.bfloat16).astype(jnp.float32)
    rest = x - high
    mid = rest.astype(jnp.bfloat16).astype(jnp.float32)
    return high, mid, rest - mid


def outer6(a, b):
    (ah, am, al), (bh, bm, bl) = a, b
    left = jnp.concatenate([ah, ah, am, am, ah, al], axis=0).astype(jnp.bfloat16)
    right = jnp.concatenate([bh, bm, bh, bm, bl, bh], axis=0).astype(jnp.bfloat16)
    return lax.dot_general(left, right, (((0,), (0,)), ((), ())), preferred_element_type=jnp.float32)


def factor_inverse(blocks, beside):
    count = len(blocks)
    beside = list(beside)
    due = [i * (count - 1) // len(beside) for i in range(len(beside))]
    mat = list(blocks)
    lane, sub = iota((8, 128), 1), iota((8, 128), 0)
    out = [jnp.where(lane == sub + 8 * i, 1.0, 0.0).astype(jnp.float32) for i in range(count)]

    def column(i, c):
        return jnp.broadcast_to(mat[i][:, c : c + 1], (8, 128))

    def apply(vectors, block):
        return tree([vectors[m] * pick(block, m) for m in range(8)])

    cols = [column(0, m) for m in range(8)]
    for k in range(count):
        invs = eliminate(cols)
        out[k] = apply(invs, out[k])
        if k + 1 == count:
            break
        done = apply(invs, mat[k])
        nxt = k + 1
        by = [column(nxt, 8 * k + m) for m in range(8)]
        factor = [tree([by[m] * pick(invs[m], j) for m in range(j + 1)]) for j in range(8)]
        if True:
            old = [column(nxt, 8 * nxt + m) for m in range(8)]
            cols = [old[m] - tree([factor[j] * pick(factor[j], m) for j in range(8)]) for m in range(8)]
        mat[nxt] = mat[nxt] - apply(factor, done)
        out[nxt] = out[nxt] - apply(factor, out[k])
        if not True:
            cols = [column(nxt, 8 * nxt + m) for m in range(8)]
        if nxt + 1 < count:
            both = thirds(jnp.concatenate([done, out[k]], axis=1))
            change = outer6([part[:, :128] for part in both], both)
            for i in range(nxt + 1, count):
                mat[i] = mat[i] - change[8 * i : 8 * i + 8, :128]
                out[i] = out[i] - change[8 * i : 8 * i + 8, 128:]
        for when, piece in zip(due, beside):
            if when == k:
                piece()
    return out


def dot6(a, b):
    (ah, am, al), (bh, bm, bl) = ([v.astype(jnp.bfloat16) for v in x] for x in (a, b))

    def part(u, v):
        return lax.dot_general(u, v, (((1,), (1,)), ((), ())), preferred_element_type=jnp.float32)

    def beside(u, v):
        return jnp.concatenate([u, v], axis=1)

    size = bh.shape[0]
    main = part(beside(ah, am), jnp.concatenate([beside(bh, bm), beside(bm, bh)], axis=0))
    return main[:, :size] + (main[:, size:] + part(beside(ah, al), beside(bl, bh)))


def remainder_kernel(
    count, sums_ref, late_ref, panel_ref, block_ref, over_hbm, coup_hbm,
    over_ref, coup_ref, panel2_ref, basis_ref, cross_ref, sem,
):
    steps = panel_ref.shape[0] // 128
    parts = 128 * steps // 512

    def early(t):
        row = jnp.concatenate([sums_ref[4 * t + b : 4 * t + b + 1, :] for b in range(4)], axis=1)
        turned = pltpu.roll(jnp.broadcast_to(row, (128, 512)), 0, 1, stride=1, stride_axis=0)
        return turned[:, 256:512], turned[:, 128:384]

    gram_top, gram_low = early(0)
    gram11 = (gram_top[:, :128] + late_ref[:128, :128]) / count
    got = {}

    def gram_rest():
        got["gram21"] = thirds((gram_low[:, :128] + late_ref[128:, :128]) / count)
        got["gram22"] = (gram_low[:, 128:] + late_ref[128:, 128:256]) / count

    def cross(t):
        def piece():
            top, low = early(t)
            cross_ref[:128, 256 * (t - 1) : 256 * t] = (top + late_ref[:128, 256 * t : 256 * t + 256]) / count
            cross_ref[128:, 256 * (t - 1) : 256 * t] = (low + late_ref[128:, 256 * t : 256 * t + 256]) / count

        return piece

    first = jnp.concatenate(
        factor_inverse(
            [gram11[8 * i : 8 * i + 8] for i in range(16)],
            [gram_rest] + [cross(1 + t) for t in range(2)],
        ),
        axis=0,
    )
    below = dot6(got["gram21"], thirds(first))
    below6 = thirds(below)
    schur = got["gram22"] - dot6(below6, below6)
    first2, below2 = split(first), split(below)

    def wide(i):
        return slice(256 * i, 256 * i + 256)

    def couple(i):
        def piece():
            coup_ref[:128, wide(i)] = dot3(first2, split(cross_ref[:128, wide(i)]))

        return piece

    def couple_rest(i):
        def piece():
            cross_ref[128:, wide(i)] = cross_ref[128:, wide(i)] - dot3(below2, split(coup_ref[:128, wide(i)]))

        return piece

    def upper(s):
        return slice(512 * s, 512 * s + 512)

    def orthogonalize(s):
        def piece():
            basis_ref[upper(s), :] = dot3(split(panel_ref[upper(s), :128]), first2, True)

        return piece

    def orthogonalize_rest(s):
        def piece():
            panel2_ref[upper(s), :] = panel_ref[upper(s), 128:] - dot3(split(basis_ref[upper(s), :]), below2, True)

        return piece

    def project(s, i):
        def piece():
            change = dot3(split(basis_ref[upper(s), :]), split(coup_ref[:128, wide(i)]))
            over_ref[upper(s), wide(i)] = block_ref[upper(s), wide(i)] - change

        return piece

    second = jnp.concatenate(
        factor_inverse(
            [schur[8 * i : 8 * i + 8] for i in range(16)],
            [couple(i) for i in range(2)]
            + [orthogonalize(s) for s in range(parts)]
            + [project(s, i) for i in range(2) for s in range(parts)]
            + [couple_rest(i) for i in range(2)]
            + [orthogonalize_rest(s) for s in range(parts)],
        ),
        axis=0,
    )
    second2 = split(second)
    basis2 = dot3(split(panel2_ref[...]), second2, True)
    basis2s = split(basis2)
    out = []
    for i in (1, 0):
        coup2 = dot3(second2, split(cross_ref[128:, wide(i)]))
        coup_ref[128:, wide(i)] = coup2
        if i == 0:
            out.append(pltpu.make_async_copy(coup_ref, coup_hbm, sem.at[2]))
            out[-1].start()
        over_ref[:, wide(i)] = over_ref[:, wide(i)] - dot3(basis2s, split(coup2))
        if i == 0:

            @pl.when(lax.axis_index("col") == 0)
            def _():
                over_ref[:, :128] = basis_ref[...]
                over_ref[:, 128:WIDE] = basis2

        out.append(pltpu.make_async_copy(over_ref.at[:, wide(i)], over_hbm.at[:, wide(i)], sem.at[i]))
        out[-1].start()
    for copy in out:
        copy.wait()


def remainder(sums, late, panel, block, count):
    rows, f32 = panel.shape[0], jnp.float32
    anywhere = pl.BlockSpec(memory_space=pl.ANY)
    return pl.pallas_call(
        functools.partial(remainder_kernel, count),
        name="remainder",
        out_shape=(jax.ShapeDtypeStruct((rows, 512), f32), jax.ShapeDtypeStruct((WIDE, 512), f32)),
        in_specs=[VM, VM, VM, VM],
        out_specs=(anywhere, anywhere),
        scratch_shapes=[
            pltpu.VMEM((rows, 512), f32),
            pltpu.VMEM((WIDE, 512), f32),
            pltpu.VMEM((rows, 128), f32),
            pltpu.VMEM((rows, 128), f32),
            pltpu.VMEM((WIDE, 512), f32),
            pltpu.SemaphoreType.DMA((3,)),
        ],
        compiler_params=pltpu.CompilerParams(vmem_limit_bytes=24 * 2**20),
    )(sums, late, panel, block)


def solution(mesh):
    slabs, cols = mesh.shape["row"] // SLAB, mesh.shape["col"]

    def body(traces):
        count = traces.shape[1] * slabs * SLAB
        held = pltpu.with_memory_space_constraint(traces, pltpu.HBM)
        return remainder(*lag_sums(held, slabs, cols), count)

    return jax.shard_map(
        body,
        mesh=mesh,
        in_specs=(P("col", "row"),),
        out_specs=(P("row", "col"), P(None, "col")),
        check_vma=False,
    )
```

```python
import functools

import jax
import jax.numpy as jnp
from jax import lax
from jax.experimental import pallas as pl
from jax.experimental.pallas import tpu as pltpu
from jax.sharding import PartitionSpec as P

TAPS = 256
WIDE = 256
SLAB = 4
MESH = pl.DeviceIdType.MESH
HIGHEST = lax.Precision.HIGHEST
VM = pl.BlockSpec(memory_space=pltpu.VMEM)


def dot(a, b, da=1, db=0):
    return lax.dot_general(
        a, b, (((da,), (db,)), ((), ())), precision=HIGHEST, preferred_element_type=jnp.float32
    )


def iota(shape, axis):
    return lax.broadcasted_iota(jnp.int32, shape, axis)


def anti_identity():
    return jnp.where(iota((128, 128), 0) + iota((128, 128), 1) == 127, 1.0, 0.0).astype(jnp.float32)


def lag_kernel(
    slabs, cols,
    x_hbm, sums_ref, late_ref, panel_ref, block_ref,
    x_ref, ext_ref, mine, own0, slab0, slabc, before0, after0, beforec, late0, latec, lags,
    local_sem, send_x, recv_x, send_0, recv_0, send_hc, recv_hc,
    send_s0, recv_s0, send_hb, recv_hb, send_ha, recv_ha, send_t, recv_t, send_l, recv_l, hello,
):
    fetch = pltpu.make_async_copy(x_hbm, x_ref, local_sem.at[1])
    fetch.start()
    row, col = lax.axis_index("row"), lax.axis_index("col")
    z, y = row // SLAB, row % SLAB
    per = x_ref.shape[1] // 128
    first, last = y == 0, y == SLAB - 1
    has_before, has_after = z > 0, z < slabs - 1
    in_tail = z == slabs - 1

    def at(zz, yy, cc):
        return (zz * SLAB + yy, cc)

    def around(k):
        return at((z + k + slabs) % slabs, y, col)

    def remote(src, dst, send, recv, where):
        return pltpu.make_async_remote_copy(
            src_ref=src, dst_ref=dst, send_sem=send, recv_sem=recv, device_id=where, device_id_type=MESH
        )

    barrier = pltpu.get_barrier_semaphore()

    def greet(where):
        pl.semaphore_signal(barrier, inc=1, device_id=where, device_id_type=MESH)

    greet(around(1))
    greet(around(-1))

    @pl.when(last & has_after)
    def _():
        for k in range(SLAB):
            greet(at(z + 1, k, col))

    @pl.when(first & has_before)
    def _():
        for k in range(SLAB):
            greet(at(z - 1, k, col))

    @pl.when(has_before)
    def _():
        greet(at(z - 1, SLAB - 1, col))

    @pl.when(has_after)
    def _():
        greet(at(z + 1, 0, col))

    @pl.when(col == 0)
    def _():
        for k in range(1, cols):
            greet(at(z, y, k))

    @pl.when(col != 0)
    def _():
        greet(at(z, y, 0))

    for k in range(1, SLAB):
        greet(at(z, (y + k) % SLAB, col))

    def yes(flag):
        return jnp.where(flag, 1, 0)

    expected = (
        2 + SLAB - 1 + yes(col != 0) + (cols - 1) * yes(col == 0)
        + SLAB * yes(last & has_after) + SLAB * yes(first & has_before)
        + yes(has_before) + yes(has_after)
    )

    @pl.when(z == 0)
    def _():
        before0[...] = jnp.zeros_like(before0)
        beforec[...] = jnp.zeros_like(beforec)

    @pl.when(in_tail)
    def _():
        after0[...] = jnp.zeros_like(after0)

    fetch.wait()
    plain = jnp.concatenate(
        [x_ref[t : t + 1, 128 * b : 128 * b + 128] for t in range(2) for b in range(per)], axis=0
    )
    turned = dot(plain, anti_identity())
    mine[...] = turned
    slabc[y] = turned

    @pl.when(col == 0)
    def _():
        own0[:per, :] = plain[:per]
        own0[per:, :] = turned[:per]

    pl.semaphore_wait(barrier, expected)

    @pl.when(col == 0)
    def _():
        for k in range(1, cols):
            remote(own0, own0, send_0.at[k], recv_0.at[0], at(z, y, k)).start()

    for k in range(1, SLAB):
        remote(mine, slabc.at[y], send_x.at[k], recv_x.at[y], at(z, (y + k) % SLAB, col)).start()

    @pl.when(last & has_after)
    def _():
        remote(mine, beforec, send_hc.at[0], recv_hc.at[0], at(z + 1, 0, col)).start()

    reach = [r for r in (1, 2, 4, 8, 16) if 4 * r <= slabs]

    def tell(i):
        for k in (reach[i], -reach[i]):
            pl.semaphore_signal(hello.at[i], inc=1, device_id=around(k), device_id_type=MESH)

    if reach:
        tell(0)
    if len(reach) > 1:
        pl.semaphore_wait(hello.at[0], 2)
        tell(1)

    @pl.when(col != 0)
    def _():
        remote(own0, own0, send_0.at[0], recv_0.at[0], at(z, y, 0)).wait_recv()

    keep_0 = pltpu.make_async_copy(own0, slab0.at[y], local_sem.at[0])
    keep_0.start()
    for k in range(1, SLAB):
        remote(own0, slab0.at[y], send_s0.at[k], recv_s0.at[y], at(z, (y + k) % SLAB, col)).start()

    @pl.when(last & has_after)
    def _():
        for k in range(SLAB):
            remote(own0, before0, send_hb.at[k], recv_hb.at[0], at(z + 1, k, col)).start()

    @pl.when(first & has_before)
    def _():
        for k in range(SLAB):
            remote(own0.at[0:2], after0, send_ha.at[k], recv_ha.at[0], at(z - 1, k, col)).start()

    for i in range(2, len(reach)):
        pl.semaphore_wait(hello.at[i - 1], 2)
        tell(i)

    keep_0.wait()
    for k in range(1, SLAB):
        other = (y + k) % SLAB
        remote(mine, slabc.at[other], send_x.at[k], recv_x.at[other], at(z, other, col)).wait_recv()
        remote(own0, slab0.at[other], send_s0.at[k], recv_s0.at[other], at(z, other, col)).wait_recv()

    @pl.when(has_before)
    def _():
        remote(own0, before0, send_hb.at[0], recv_hb.at[0], at(z, y, col)).wait_recv()

    @pl.when(has_after)
    def _():
        remote(own0.at[0:2], after0, send_ha.at[0], recv_ha.at[0], at(z, y, col)).wait_recv()

    def all_came():
        if reach:
            pl.semaphore_wait(hello.at[len(reach) - 1], 2)

    def tails(k):
        return (
            remote(slab0.at[SLAB - 1, per - 2 : per], late0, send_t.at[0, k], recv_t.at[0], around(k)),
            remote(slabc.at[SLAB - 1, per - 2 : per], latec.at[0], send_t.at[1, k], recv_t.at[1], around(k)),
            remote(slabc.at[SLAB - 1, 2 * per - 2 :], latec.at[1], send_t.at[2, k], recv_t.at[2], around(k)),
        )

    @pl.when(in_tail)
    def _():
        all_came()

        @pl.loop(1, slabs)
        def _(k):
            for copy in tails(k):
                copy.start()

        late0[...] = slab0[SLAB - 1, per - 2 : per]
        latec[0] = slabc[SLAB - 1, per - 2 : per]
        latec[1] = slabc[SLAB - 1, 2 * per - 2 :]

    count = SLAB * per
    ext0 = jnp.concatenate([before0[per - 2 : per, :]] + [slab0[j, :per, :] for j in range(SLAB)] + [after0[...]], axis=0)
    wide0 = jnp.concatenate([ext0[k : k + count] for k in range(5)], axis=1)
    place = iota((count, 640), 0) * 128 + iota((count, 640), 1) - 256
    late = count * 128 - (TAPS - 1)
    wide0_early = jnp.where(in_tail & (place >= late), 0.0, wide0)
    right = jnp.concatenate([wide0, wide0_early[count - 8 :]], axis=0)
    at_late = in_tail & (iota((count, 128), 0) * 128 + 127 - iota((count, 128), 1) >= late)
    lefts = []
    for t in range(3):
        if t == 0:
            group = jnp.concatenate([slab0[j, per:, :] for j in range(SLAB)], axis=0)
        else:
            group = jnp.concatenate([slabc[j, per * (t - 1) : per * t, :] for j in range(SLAB)], axis=0)
        lefts.append(
            jnp.concatenate([jnp.where(at_late, 0.0, group), jnp.where(at_late, group, 0.0)[count - 8 :]], axis=0)
        )
    table = outer6(thirds(jnp.concatenate(lefts, axis=1)), thirds(right))
    for t in range(3):
        skewed = pltpu.roll(table[128 * t : 128 * t + 128], min(t, 1), 1, stride=1, stride_axis=0)
        summed = jnp.sum(skewed, axis=0, keepdims=True)
        at_row = max(4 * t - 2, 0)
        for b in range(2 if t == 0 else 4):
            lags[z, at_row + b : at_row + b + 1, :] = summed[:, 128 + 128 * b : 256 + 128 * b]

    def exchange(k):
        return remote(lags.at[z], lags.at[z], send_l.at[k], recv_l.at[0], around(k))

    pl.when(z < slabs - 1)(all_came)

    @pl.loop(0, slabs - 1)
    def _(k):
        exchange(1 + (k + slabs // 2 - 1) % (slabs - 1)).start()

    reach_back = per + 2
    ext_ref[2:reach_back, :] = own0[per:, :]
    for t in range(2):
        ext_ref[reach_back * (t + 1) + 2 : reach_back * (t + 2), :] = mine[per * t : per * t + per, :]

    @pl.when(first)
    def _():
        @pl.when(has_before)
        def _():
            remote(mine, beforec, send_hc.at[0], recv_hc.at[0], at(z, y, col)).wait_recv()

        ext_ref[0:2, :] = before0[2 * per - 2 :, :]
        for t in range(2):
            ext_ref[reach_back * (t + 1) : reach_back * (t + 1) + 2, :] = beforec[per * t + per - 2 : per * t + per, :]

    @pl.when(y > 0)
    def _():
        before = (y + SLAB - 1) % SLAB
        ext_ref[0:2, :] = slab0[before, 2 * per - 2 :, :]
        for t in range(2):
            ext_ref[reach_back * (t + 1) : reach_back * (t + 1) + 2, :] = slabc[before, per * t + per - 2 : per * t + per, :]

    for t in range(3):
        line = jnp.concatenate(
            [ext_ref[reach_back * t + b : reach_back * t + b + 1, :] for b in reversed(range(reach_back))], axis=1
        )
        spun = pltpu.roll(jnp.broadcast_to(line, (128, 128 * reach_back)), 1, 1, stride=1, stride_axis=0)
        for k in range(2):
            for s in range(per):
                block = spun[:, 512 + 128 * (k - s) : 640 + 128 * (k - s)]
                if t == 0:
                    panel_ref[128 * s : 128 * s + 128, 128 * k : 128 * k + 128] = block
                else:
                    block_ref[128 * s : 128 * s + 128, 256 * (t - 1) + 128 * k : 256 * (t - 1) + 128 * k + 128] = block

    @pl.when(z < slabs - 1)
    def _():
        for copy in tails(0):
            copy.wait_recv()

    ends = jnp.concatenate([latec[0], latec[1], jnp.zeros((4, 128), jnp.float32)], axis=0)
    forward = dot(ends, anti_identity())

    def late_rows(t):
        rows = late0[...] if t == 0 else forward[2 * t - 2 : 2 * t]
        tail = jnp.where(iota((1, TAPS), 1) == 0, 0.0, jnp.concatenate([rows[0:1], rows[1:2]], axis=1))
        line = jnp.concatenate([jnp.zeros((1, 128), jnp.float32), tail], axis=1)
        spun = pltpu.roll(jnp.broadcast_to(line, (128, 384)), 0, 1, stride=1, stride_axis=0)
        return spun[:, 128:256], spun[:, 256:384]

    near0, far0 = late_rows(0)
    near6, far6 = thirds(near0), thirds(far0)
    near_near = dot6(near6, near6)
    late_ref[:128, :128] = near_near + dot6(far6, far6)
    late_ref[128:, :128] = dot6(near6, far6)
    late_ref[128:, 128:256] = near_near
    near_a, far_a = split(near0), split(far0)
    for t in (1, 2):
        near_c, far_c = (split(v) for v in late_rows(t))
        same = dot3(near_a, near_c, True)
        late_ref[:128, 256 * t : 256 * t + 128] = same + dot3(far_a, far_c, True)
        late_ref[:128, 256 * t + 128 : 256 * t + 256] = dot3(far_a, near_c, True)
        late_ref[128:, 256 * t : 256 * t + 128] = dot3(near_a, far_c, True)
        late_ref[128:, 256 * t + 128 : 256 * t + 256] = same

    @pl.when(col == 0)
    def _():
        for k in range(1, cols):
            remote(own0, own0, send_0.at[k], recv_0.at[0], at(z, y, k)).wait_send()

    for k in range(1, SLAB):
        other = (y + k) % SLAB
        remote(mine, slabc.at[y], send_x.at[k], recv_x.at[y], at(z, other, col)).wait_send()
        remote(own0, slab0.at[y], send_s0.at[k], recv_s0.at[y], at(z, other, col)).wait_send()

    @pl.when(last & has_after)
    def _():
        remote(mine, beforec, send_hc.at[0], recv_hc.at[0], at(z + 1, 0, col)).wait_send()
        for k in range(SLAB):
            remote(own0, before0, send_hb.at[k], recv_hb.at[0], at(z + 1, k, col)).wait_send()

    @pl.when(first & has_before)
    def _():
        for k in range(SLAB):
            remote(own0.at[0:2], after0, send_ha.at[k], recv_ha.at[0], at(z - 1, k, col)).wait_send()

    @pl.when(in_tail)
    def _():
        @pl.loop(1, slabs)
        def _(k):
            for copy in tails(k):
                copy.wait_send()

    @pl.loop(1, slabs)
    def _(k):
        exchange(k).wait_send()

    others = lags.at[pl.ds(0, slabs - 1)]
    remote(others, others, send_l.at[0], recv_l.at[0], around(1)).wait_recv()

    sums_ref[...] = tree([lags[k] for k in range(slabs)])


def lag_sums(traces, slabs, cols):
    rows = traces.shape[1]
    per = rows // 128
    f32, dma = jnp.float32, pltpu.SemaphoreType.DMA
    return pl.pallas_call(
        functools.partial(lag_kernel, slabs, cols),
        name="lag_sums",
        out_shape=(
            jax.ShapeDtypeStruct((10, 128), f32),
            jax.ShapeDtypeStruct((WIDE, WIDE + 2 * TAPS), f32),
            jax.ShapeDtypeStruct((rows, WIDE), f32),
            jax.ShapeDtypeStruct((rows, 2 * TAPS), f32),
        ),
        in_specs=[pl.BlockSpec(memory_space=pltpu.HBM)],
        out_specs=(VM, VM, VM, VM),
        scratch_shapes=[
            pltpu.VMEM((2, rows), f32),
            pltpu.VMEM((3 * (per + 2), 128), f32),
            pltpu.VMEM((2 * per, 128), f32),
            pltpu.VMEM((2 * per, 128), f32),
            pltpu.VMEM((SLAB, 2 * per, 128), f32),
            pltpu.VMEM((SLAB, 2 * per, 128), f32),
            pltpu.VMEM((2 * per, 128), f32),
            pltpu.VMEM((2, 128), f32),
            pltpu.VMEM((2 * per, 128), f32),
            pltpu.VMEM((2, 128), f32),
            pltpu.VMEM((2, 2, 128), f32),
            pltpu.VMEM((slabs, 10, 128), f32),
            dma((2,)),
            dma((SLAB,)), dma((SLAB,)),
            dma((cols,)), dma((1,)),
            dma((1,)), dma((1,)),
            dma((SLAB,)), dma((SLAB,)),
            dma((SLAB,)), dma((1,)),
            dma((SLAB,)), dma((1,)),
            dma((3, slabs)), dma((3,)),
            dma((slabs,)), dma((slabs,)),
            pltpu.SemaphoreType.REGULAR((5,)),
        ],
        compiler_params=pltpu.CompilerParams(
            collective_id=0, has_side_effects=True, vmem_limit_bytes=12 * 2**20
        ),
    )(traces)


def split(x):
    high = x.astype(jnp.bfloat16)
    return high, (x - high.astype(jnp.float32)).astype(jnp.bfloat16)


def dot3(a, b, nt=False):
    (ah, al), (bh, bl) = a, b
    left = jnp.concatenate([ah, al, ah], axis=1)
    right = jnp.concatenate([bh, bh, bl], axis=1 if nt else 0)
    return lax.dot_general(
        left, right, (((1,), (1 if nt else 0,)), ((), ())), preferred_element_type=jnp.float32
    )


def tree(terms):
    while len(terms) > 1:
        terms = [terms[i] + terms[i + 1] if i + 1 < len(terms) else terms[i] for i in range(0, len(terms), 2)]
    return terms[0]


def pick(v, j):
    return jnp.broadcast_to(v[j : j + 1], (8, 128))


def eliminate(cols):
    sub = iota((8, 128), 0)
    cols = list(cols)
    invs = [jnp.where(sub == j, 1.0, 0.0).astype(jnp.float32) for j in range(8)]
    scales = None
    for j in range(8):
        scale = lax.rsqrt(pick(cols[j], j))
        scales = scale if scales is None else jnp.where(sub == j, scale, scales)
        if j == 7:
            break
        below = jnp.where(sub > j, cols[j], 0.0)
        square = scale * scale
        ratio = below * square
        cols[j + 1] = cols[j + 1] - (below * pick(cols[j + 1], j)) * square
        for m in range(j + 2, 8):
            cols[m] = cols[m] - ratio * pick(cols[m], j)
        for m in range(j):
            invs[m] = invs[m] - ratio * pick(invs[m], j)
        invs[j] = invs[j] - ratio
    return [v * scales for v in invs]


def thirds(x):
    high = x.astype(jnp.bfloat16).astype(jnp.float32)
    rest = x - high
    mid = rest.astype(jnp.bfloat16).astype(jnp.float32)
    return high, mid, rest - mid


def outer6(a, b):
    (ah, am, al), (bh, bm, bl) = a, b
    left = jnp.concatenate([ah, ah, am, am, ah, al], axis=0).astype(jnp.bfloat16)
    right = jnp.concatenate([bh, bm, bh, bm, bl, bh], axis=0).astype(jnp.bfloat16)
    return lax.dot_general(left, right, (((0,), (0,)), ((), ())), preferred_element_type=jnp.float32)


def factor_inverse(blocks, beside):
    count = len(blocks)
    beside = list(beside)
    due = [i * (count - 1) // len(beside) for i in range(len(beside))]
    mat = list(blocks)
    lane, sub = iota((8, 128), 1), iota((8, 128), 0)
    out = [jnp.where(lane == sub + 8 * i, 1.0, 0.0).astype(jnp.float32) for i in range(count)]

    def column(i, c):
        return jnp.broadcast_to(mat[i][:, c : c + 1], (8, 128))

    def apply(vectors, block):
        return tree([vectors[m] * pick(block, m) for m in range(8)])

    cols = [column(0, m) for m in range(8)]
    for k in range(count):
        invs = eliminate(cols)
        out[k] = apply(invs, out[k])
        if k + 1 == count:
            break
        done = apply(invs, mat[k])
        nxt = k + 1
        by = [column(nxt, 8 * k + m) for m in range(8)]
        factor = [tree([by[m] * pick(invs[m], j) for m in range(j + 1)]) for j in range(8)]
        if True:
            old = [column(nxt, 8 * nxt + m) for m in range(8)]
            cols = [old[m] - tree([factor[j] * pick(factor[j], m) for j in range(8)]) for m in range(8)]
        mat[nxt] = mat[nxt] - apply(factor, done)
        out[nxt] = out[nxt] - apply(factor, out[k])
        if not True:
            cols = [column(nxt, 8 * nxt + m) for m in range(8)]
        if nxt + 1 < count:
            both = thirds(jnp.concatenate([done, out[k]], axis=1))
            change = outer6([part[:, :128] for part in both], both)
            for i in range(nxt + 1, count):
                mat[i] = mat[i] - change[8 * i : 8 * i + 8, :128]
                out[i] = out[i] - change[8 * i : 8 * i + 8, 128:]
        for when, piece in zip(due, beside):
            if when == k:
                piece()
    return out


def dot6(a, b):
    (ah, am, al), (bh, bm, bl) = ([v.astype(jnp.bfloat16) for v in x] for x in (a, b))

    def part(u, v):
        return lax.dot_general(u, v, (((1,), (1,)), ((), ())), preferred_element_type=jnp.float32)

    def beside(u, v):
        return jnp.concatenate([u, v], axis=1)

    size = bh.shape[0]
    main = part(beside(ah, am), jnp.concatenate([beside(bh, bm), beside(bm, bh)], axis=0))
    return main[:, :size] + (main[:, size:] + part(beside(ah, al), beside(bl, bh)))


def remainder_kernel(
    count, sums_ref, late_ref, panel_ref, block_ref, over_hbm, coup_hbm,
    over_ref, coup_ref, panel2_ref, basis_ref, cross_ref, sem,
):
    steps = panel_ref.shape[0] // 128
    parts = 128 * steps // 512

    def early(t):
        row = jnp.concatenate([sums_ref[4 * t - 2 + b : 4 * t - 1 + b, :] for b in range(4)], axis=1)
        turned = pltpu.roll(jnp.broadcast_to(row, (128, 512)), 0, 1, stride=1, stride_axis=0)
        return turned[:, 256:512], turned[:, 128:384]

    half = jnp.concatenate([sums_ref[0:1, :], sums_ref[1:2, :], jnp.zeros((1, 128), jnp.float32)], axis=1)
    spun = pltpu.roll(jnp.broadcast_to(half, (128, 384)), 1, 1, stride=1, stride_axis=0)
    below_diagonal = spun[:, 256:384]
    gram_near = jnp.where(
        iota((128, 128), 0) >= iota((128, 128), 1), below_diagonal, jnp.transpose(below_diagonal)
    )
    gram11 = (gram_near + late_ref[:128, :128]) / count
    got = {}

    def gram_rest():
        got["gram21"] = thirds((spun[:, 128:256] + late_ref[128:, :128]) / count)
        got["gram22"] = (gram_near + late_ref[128:, 128:256]) / count

    def cross(t):
        def piece():
            top, low = early(t)
            cross_ref[:128, 256 * (t - 1) : 256 * t] = (top + late_ref[:128, 256 * t : 256 * t + 256]) / count
            cross_ref[128:, 256 * (t - 1) : 256 * t] = (low + late_ref[128:, 256 * t : 256 * t + 256]) / count

        return piece

    first = jnp.concatenate(
        factor_inverse(
            [gram11[8 * i : 8 * i + 8] for i in range(16)],
            [gram_rest] + [cross(1 + t) for t in range(2)],
        ),
        axis=0,
    )
    below = dot6(got["gram21"], thirds(first))
    below6 = thirds(below)
    schur = got["gram22"] - dot6(below6, below6)
    first2, below2 = split(first), split(below)

    def wide(i):
        return slice(256 * i, 256 * i + 256)

    def couple(i):
        def piece():
            coup_ref[:128, wide(i)] = dot3(first2, split(cross_ref[:128, wide(i)]))

        return piece

    def couple_rest(i):
        def piece():
            cross_ref[128:, wide(i)] = cross_ref[128:, wide(i)] - dot3(below2, split(coup_ref[:128, wide(i)]))

        return piece

    def upper(s):
        return slice(512 * s, 512 * s + 512)

    def orthogonalize(s):
        def piece():
            basis_ref[upper(s), :] = dot3(split(panel_ref[upper(s), :128]), first2, True)

        return piece

    def orthogonalize_rest(s):
        def piece():
            panel2_ref[upper(s), :] = panel_ref[upper(s), 128:] - dot3(split(basis_ref[upper(s), :]), below2, True)

        return piece

    def project(s, i):
        def piece():
            change = dot3(split(basis_ref[upper(s), :]), split(coup_ref[:128, wide(i)]))
            over_ref[upper(s), wide(i)] = block_ref[upper(s), wide(i)] - change

        return piece

    second = jnp.concatenate(
        factor_inverse(
            [schur[8 * i : 8 * i + 8] for i in range(16)],
            [couple(i) for i in range(2)]
            + [orthogonalize(s) for s in range(parts)]
            + [project(s, i) for i in range(2) for s in range(parts)]
            + [couple_rest(i) for i in range(2)]
            + [orthogonalize_rest(s) for s in range(parts)],
        ),
        axis=0,
    )
    second2 = split(second)
    basis2 = dot3(split(panel2_ref[...]), second2, True)
    basis2s = split(basis2)
    out = []
    for i in (1, 0):
        coup2 = dot3(second2, split(cross_ref[128:, wide(i)]))
        coup_ref[128:, wide(i)] = coup2
        if i == 0:
            out.append(pltpu.make_async_copy(coup_ref, coup_hbm, sem.at[2]))
            out[-1].start()
        over_ref[:, wide(i)] = over_ref[:, wide(i)] - dot3(basis2s, split(coup2))
        if i == 0:

            @pl.when(lax.axis_index("col") == 0)
            def _():
                over_ref[:, :128] = basis_ref[...]
                over_ref[:, 128:WIDE] = basis2

        out.append(pltpu.make_async_copy(over_ref.at[:, wide(i)], over_hbm.at[:, wide(i)], sem.at[i]))
        out[-1].start()
    for copy in out:
        copy.wait()


def remainder(sums, late, panel, block, count):
    rows, f32 = panel.shape[0], jnp.float32
    anywhere = pl.BlockSpec(memory_space=pl.ANY)
    return pl.pallas_call(
        functools.partial(remainder_kernel, count),
        name="remainder",
        out_shape=(jax.ShapeDtypeStruct((rows, 512), f32), jax.ShapeDtypeStruct((WIDE, 512), f32)),
        in_specs=[VM, VM, VM, VM],
        out_specs=(anywhere, anywhere),
        scratch_shapes=[
            pltpu.VMEM((rows, 512), f32),
            pltpu.VMEM((WIDE, 512), f32),
            pltpu.VMEM((rows, 128), f32),
            pltpu.VMEM((rows, 128), f32),
            pltpu.VMEM((WIDE, 512), f32),
            pltpu.SemaphoreType.DMA((3,)),
        ],
        compiler_params=pltpu.CompilerParams(vmem_limit_bytes=24 * 2**20),
    )(sums, late, panel, block)


def solution(mesh):
    slabs, cols = mesh.shape["row"] // SLAB, mesh.shape["col"]

    def body(traces):
        count = traces.shape[1] * slabs * SLAB
        held = pltpu.with_memory_space_constraint(traces, pltpu.HBM)
        return remainder(*lag_sums(held, slabs, cols), count)

    return jax.shard_map(
        body,
        mesh=mesh,
        in_specs=(P("col", "row"),),
        out_specs=(P("row", "col"), P(None, "col")),
        check_vma=False,
    )
```

```python
import functools

import jax
import jax.numpy as jnp
from jax import lax
from jax.experimental import pallas as pl
from jax.experimental.pallas import tpu as pltpu
from jax.sharding import PartitionSpec as P

TAPS = 256
WIDE = 256
SLAB = 4
MESH = pl.DeviceIdType.MESH
HIGHEST = lax.Precision.HIGHEST
VM = pl.BlockSpec(memory_space=pltpu.VMEM)


def dot(a, b, da=1, db=0):
    return lax.dot_general(
        a, b, (((da,), (db,)), ((), ())), precision=HIGHEST, preferred_element_type=jnp.float32
    )


def iota(shape, axis):
    return lax.broadcasted_iota(jnp.int32, shape, axis)


def anti_identity():
    return jnp.where(iota((128, 128), 0) + iota((128, 128), 1) == 127, 1.0, 0.0).astype(jnp.float32)


def lag_kernel(
    slabs, cols,
    x_hbm, sums_ref, late_ref, panel_ref, block_ref,
    x_ref, ext_ref, mine, own0, slab0, slabc, before0, after0, beforec, late0, latec, lags,
    local_sem, send_x, recv_x, send_0, recv_0, send_hc, recv_hc,
    send_s0, recv_s0, send_hb, recv_hb, send_ha, recv_ha, send_t, recv_t, send_l, recv_l, hello,
):
    fetch = pltpu.make_async_copy(x_hbm, x_ref, local_sem.at[1])
    fetch.start()
    row, col = lax.axis_index("row"), lax.axis_index("col")
    z, y = row // SLAB, row % SLAB
    per = x_ref.shape[1] // 128
    first, last = y == 0, y == SLAB - 1
    has_before, has_after = z > 0, z < slabs - 1
    in_tail = z == slabs - 1

    def at(zz, yy, cc):
        return (zz * SLAB + yy, cc)

    def around(k):
        return at((z + k + slabs) % slabs, y, col)

    def remote(src, dst, send, recv, where):
        return pltpu.make_async_remote_copy(
            src_ref=src, dst_ref=dst, send_sem=send, recv_sem=recv, device_id=where, device_id_type=MESH
        )

    barrier = pltpu.get_barrier_semaphore()

    def greet(where):
        pl.semaphore_signal(barrier, inc=1, device_id=where, device_id_type=MESH)

    greet(around(1))
    greet(around(-1))

    @pl.when(last & has_after)
    def _():
        for k in range(SLAB):
            greet(at(z + 1, k, col))

    @pl.when(first & has_before)
    def _():
        for k in range(SLAB):
            greet(at(z - 1, k, col))

    @pl.when(has_before)
    def _():
        greet(at(z - 1, SLAB - 1, col))

    @pl.when(has_after)
    def _():
        greet(at(z + 1, 0, col))

    @pl.when(col == 0)
    def _():
        for k in range(1, cols):
            greet(at(z, y, k))

    @pl.when(col != 0)
    def _():
        greet(at(z, y, 0))

    for k in range(1, SLAB):
        greet(at(z, (y + k) % SLAB, col))

    def yes(flag):
        return jnp.where(flag, 1, 0)

    expected = (
        2 + SLAB - 1 + yes(col != 0) + (cols - 1) * yes(col == 0)
        + SLAB * yes(last & has_after) + SLAB * yes(first & has_before)
        + yes(has_before) + yes(has_after)
    )

    @pl.when(z == 0)
    def _():
        before0[...] = jnp.zeros_like(before0)
        beforec[...] = jnp.zeros_like(beforec)

    @pl.when(in_tail)
    def _():
        after0[...] = jnp.zeros_like(after0)

    fetch.wait()
    plain = jnp.concatenate(
        [x_ref[t : t + 1, 128 * b : 128 * b + 128] for t in range(2) for b in range(per)], axis=0
    )
    turned = dot(plain, anti_identity())
    mine[...] = turned
    slabc[y] = turned

    @pl.when(col == 0)
    def _():
        own0[:per, :] = plain[:per]
        own0[per:, :] = turned[:per]

    pl.semaphore_wait(barrier, expected)

    @pl.when(col == 0)
    def _():
        for k in range(1, cols):
            remote(own0, own0, send_0.at[k], recv_0.at[0], at(z, y, k)).start()

    for k in range(1, SLAB):
        remote(mine, slabc.at[y], send_x.at[k], recv_x.at[y], at(z, (y + k) % SLAB, col)).start()

    @pl.when(last & has_after)
    def _():
        remote(mine, beforec, send_hc.at[0], recv_hc.at[0], at(z + 1, 0, col)).start()

    reach = [r for r in (1, 2, 4, 8, 16) if 4 * r <= slabs]

    def tell(i):
        for k in (reach[i], -reach[i]):
            pl.semaphore_signal(hello.at[i], inc=1, device_id=around(k), device_id_type=MESH)

    if reach:
        tell(0)
    if len(reach) > 1:
        pl.semaphore_wait(hello.at[0], 2)
        tell(1)

    @pl.when(col != 0)
    def _():
        remote(own0, own0, send_0.at[0], recv_0.at[0], at(z, y, 0)).wait_recv()

    keep_0 = pltpu.make_async_copy(own0, slab0.at[y], local_sem.at[0])
    keep_0.start()
    for k in range(1, SLAB):
        remote(own0, slab0.at[y], send_s0.at[k], recv_s0.at[y], at(z, (y + k) % SLAB, col)).start()

    @pl.when(last & has_after)
    def _():
        for k in range(SLAB):
            remote(own0, before0, send_hb.at[k], recv_hb.at[0], at(z + 1, k, col)).start()

    @pl.when(first & has_before)
    def _():
        for k in range(SLAB):
            remote(own0.at[0:2], after0, send_ha.at[k], recv_ha.at[0], at(z - 1, k, col)).start()

    for i in range(2, len(reach)):
        pl.semaphore_wait(hello.at[i - 1], 2)
        tell(i)

    keep_0.wait()
    for k in range(1, SLAB):
        other = (y + k) % SLAB
        remote(mine, slabc.at[other], send_x.at[k], recv_x.at[other], at(z, other, col)).wait_recv()
        remote(own0, slab0.at[other], send_s0.at[k], recv_s0.at[other], at(z, other, col)).wait_recv()

    @pl.when(has_before)
    def _():
        remote(own0, before0, send_hb.at[0], recv_hb.at[0], at(z, y, col)).wait_recv()

    @pl.when(has_after)
    def _():
        remote(own0.at[0:2], after0, send_ha.at[0], recv_ha.at[0], at(z, y, col)).wait_recv()

    def all_came():
        if reach:
            pl.semaphore_wait(hello.at[len(reach) - 1], 2)

    def tails(k):
        return (
            remote(slab0.at[SLAB - 1, per - 2 : per], late0, send_t.at[0, k], recv_t.at[0], around(k)),
            remote(slabc.at[SLAB - 1, per - 2 : per], latec.at[0], send_t.at[1, k], recv_t.at[1], around(k)),
            remote(slabc.at[SLAB - 1, 2 * per - 2 :], latec.at[1], send_t.at[2, k], recv_t.at[2], around(k)),
        )

    @pl.when(in_tail)
    def _():
        all_came()

        @pl.loop(1, slabs)
        def _(k):
            for copy in tails(k):
                copy.start()

        late0[...] = slab0[SLAB - 1, per - 2 : per]
        latec[0] = slabc[SLAB - 1, per - 2 : per]
        latec[1] = slabc[SLAB - 1, 2 * per - 2 :]

    count = SLAB * per
    ext0 = jnp.concatenate([before0[per - 2 : per, :]] + [slab0[j, :per, :] for j in range(SLAB)] + [after0[...]], axis=0)
    wide0 = jnp.concatenate([ext0[k : k + count] for k in range(5)], axis=1)
    place = iota((count, 640), 0) * 128 + iota((count, 640), 1) - 256
    late = count * 128 - (TAPS - 1)
    wide0_early = jnp.where(in_tail & (place >= late), 0.0, wide0)
    right = jnp.concatenate([wide0, wide0_early[count - 8 :]], axis=0)
    at_late = in_tail & (iota((count, 128), 0) * 128 + 127 - iota((count, 128), 1) >= late)
    lefts = []
    for t in range(3):
        if t == 0:
            group = jnp.concatenate([slab0[j, per:, :] for j in range(SLAB)], axis=0)
        else:
            group = jnp.concatenate([slabc[j, per * (t - 1) : per * t, :] for j in range(SLAB)], axis=0)
        lefts.append(
            jnp.concatenate([jnp.where(at_late, 0.0, group), jnp.where(at_late, group, 0.0)[count - 8 :]], axis=0)
        )
    table = outer6(thirds(jnp.concatenate(lefts, axis=1)), thirds(right))
    for t in range(3):
        skewed = pltpu.roll(table[128 * t : 128 * t + 128], min(t, 1), 1, stride=1, stride_axis=0)
        summed = jnp.sum(skewed, axis=0, keepdims=True)
        at_row = max(4 * t - 2, 0)
        for b in range(2 if t == 0 else 4):
            lags[z, at_row + b : at_row + b + 1, :] = summed[:, 128 + 128 * b : 256 + 128 * b]

    def exchange(k):
        return remote(lags.at[z], lags.at[z], send_l.at[k], recv_l.at[0], around(k))

    pl.when(z < slabs - 1)(all_came)

    @pl.loop(0, slabs - 1)
    def _(k):
        exchange(1 + (k + slabs // 2 - 1) % (slabs - 1)).start()

    reach_back = per + 2
    ext_ref[2:reach_back, :] = own0[per:, :]
    for t in range(2):
        ext_ref[reach_back * (t + 1) + 2 : reach_back * (t + 2), :] = mine[per * t : per * t + per, :]

    @pl.when(first)
    def _():
        @pl.when(has_before)
        def _():
            remote(mine, beforec, send_hc.at[0], recv_hc.at[0], at(z, y, col)).wait_recv()

        ext_ref[0:2, :] = before0[2 * per - 2 :, :]
        for t in range(2):
            ext_ref[reach_back * (t + 1) : reach_back * (t + 1) + 2, :] = beforec[per * t + per - 2 : per * t + per, :]

    @pl.when(y > 0)
    def _():
        before = (y + SLAB - 1) % SLAB
        ext_ref[0:2, :] = slab0[before, 2 * per - 2 :, :]
        for t in range(2):
            ext_ref[reach_back * (t + 1) : reach_back * (t + 1) + 2, :] = slabc[before, per * t + per - 2 : per * t + per, :]

    for t in range(3):
        line = jnp.concatenate(
            [ext_ref[reach_back * t + b : reach_back * t + b + 1, :] for b in reversed(range(reach_back))], axis=1
        )
        spun = pltpu.roll(jnp.broadcast_to(line, (128, 128 * reach_back)), 1, 1, stride=1, stride_axis=0)
        for k in range(2):
            for s in range(per):
                block = spun[:, 512 + 128 * (k - s) : 640 + 128 * (k - s)]
                if t == 0:
                    panel_ref[128 * s : 128 * s + 128, 128 * k : 128 * k + 128] = block
                else:
                    block_ref[128 * s : 128 * s + 128, 256 * (t - 1) + 128 * k : 256 * (t - 1) + 128 * k + 128] = block

    @pl.when(z < slabs - 1)
    def _():
        for copy in tails(0):
            copy.wait_recv()

    ends = jnp.concatenate([latec[0], latec[1], jnp.zeros((4, 128), jnp.float32)], axis=0)
    forward = dot(ends, anti_identity())

    def late_rows(t):
        rows = late0[...] if t == 0 else forward[2 * t - 2 : 2 * t]
        tail = jnp.where(iota((1, TAPS), 1) == 0, 0.0, jnp.concatenate([rows[0:1], rows[1:2]], axis=1))
        line = jnp.concatenate([jnp.zeros((1, 128), jnp.float32), tail], axis=1)
        spun = pltpu.roll(jnp.broadcast_to(line, (128, 384)), 0, 1, stride=1, stride_axis=0)
        return spun[:, 128:256], spun[:, 256:384]

    near0, far0 = late_rows(0)
    near6, far6 = thirds(near0), thirds(far0)
    near_near = dot6(near6, near6)
    late_ref[:128, :128] = near_near + dot6(far6, far6)
    late_ref[128:, :128] = dot6(near6, far6)
    late_ref[128:, 128:256] = near_near
    near_a, far_a = split(near0), split(far0)
    for t in (1, 2):
        near_c, far_c = (split(v) for v in late_rows(t))
        same = dot3(near_a, near_c, True)
        late_ref[:128, 256 * t : 256 * t + 128] = same + dot3(far_a, far_c, True)
        late_ref[:128, 256 * t + 128 : 256 * t + 256] = dot3(far_a, near_c, True)
        late_ref[128:, 256 * t : 256 * t + 128] = dot3(near_a, far_c, True)
        late_ref[128:, 256 * t + 128 : 256 * t + 256] = same

    @pl.when(col == 0)
    def _():
        for k in range(1, cols):
            remote(own0, own0, send_0.at[k], recv_0.at[0], at(z, y, k)).wait_send()

    for k in range(1, SLAB):
        other = (y + k) % SLAB
        remote(mine, slabc.at[y], send_x.at[k], recv_x.at[y], at(z, other, col)).wait_send()
        remote(own0, slab0.at[y], send_s0.at[k], recv_s0.at[y], at(z, other, col)).wait_send()

    @pl.when(last & has_after)
    def _():
        remote(mine, beforec, send_hc.at[0], recv_hc.at[0], at(z + 1, 0, col)).wait_send()
        for k in range(SLAB):
            remote(own0, before0, send_hb.at[k], recv_hb.at[0], at(z + 1, k, col)).wait_send()

    @pl.when(first & has_before)
    def _():
        for k in range(SLAB):
            remote(own0.at[0:2], after0, send_ha.at[k], recv_ha.at[0], at(z - 1, k, col)).wait_send()

    @pl.when(in_tail)
    def _():
        @pl.loop(1, slabs)
        def _(k):
            for copy in tails(k):
                copy.wait_send()

    @pl.loop(1, slabs)
    def _(k):
        exchange(k).wait_send()

    others = lags.at[pl.ds(0, slabs - 1)]
    remote(others, others, send_l.at[0], recv_l.at[0], around(1)).wait_recv()

    sums_ref[...] = tree([lags[k] for k in range(slabs)])


def lag_sums(traces, slabs, cols):
    rows = traces.shape[1]
    per = rows // 128
    f32, dma = jnp.float32, pltpu.SemaphoreType.DMA
    return pl.pallas_call(
        functools.partial(lag_kernel, slabs, cols),
        name="lag_sums",
        out_shape=(
            jax.ShapeDtypeStruct((10, 128), f32),
            jax.ShapeDtypeStruct((WIDE, WIDE + 2 * TAPS), f32),
            jax.ShapeDtypeStruct((rows, WIDE), f32),
            jax.ShapeDtypeStruct((rows, 2 * TAPS), f32),
        ),
        in_specs=[pl.BlockSpec(memory_space=pltpu.HBM)],
        out_specs=(VM, VM, VM, VM),
        scratch_shapes=[
            pltpu.VMEM((2, rows), f32),
            pltpu.VMEM((3 * (per + 2), 128), f32),
            pltpu.VMEM((2 * per, 128), f32),
            pltpu.VMEM((2 * per, 128), f32),
            pltpu.VMEM((SLAB, 2 * per, 128), f32),
            pltpu.VMEM((SLAB, 2 * per, 128), f32),
            pltpu.VMEM((2 * per, 128), f32),
            pltpu.VMEM((2, 128), f32),
            pltpu.VMEM((2 * per, 128), f32),
            pltpu.VMEM((2, 128), f32),
            pltpu.VMEM((2, 2, 128), f32),
            pltpu.VMEM((slabs, 10, 128), f32),
            dma((2,)),
            dma((SLAB,)), dma((SLAB,)),
            dma((cols,)), dma((1,)),
            dma((1,)), dma((1,)),
            dma((SLAB,)), dma((SLAB,)),
            dma((SLAB,)), dma((1,)),
            dma((SLAB,)), dma((1,)),
            dma((3, slabs)), dma((3,)),
            dma((slabs,)), dma((slabs,)),
            pltpu.SemaphoreType.REGULAR((5,)),
        ],
        compiler_params=pltpu.CompilerParams(
            collective_id=0, has_side_effects=True, vmem_limit_bytes=12 * 2**20
        ),
    )(traces)


def split(x):
    high = x.astype(jnp.bfloat16)
    return high, (x - high.astype(jnp.float32)).astype(jnp.bfloat16)


def dot3(a, b, nt=False):
    (ah, al), (bh, bl) = a, b
    left = jnp.concatenate([ah, al, ah], axis=1)
    right = jnp.concatenate([bh, bh, bl], axis=1 if nt else 0)
    return lax.dot_general(
        left, right, (((1,), (1 if nt else 0,)), ((), ())), preferred_element_type=jnp.float32
    )


def tree(terms):
    while len(terms) > 1:
        terms = [terms[i] + terms[i + 1] if i + 1 < len(terms) else terms[i] for i in range(0, len(terms), 2)]
    return terms[0]


def pick(v, j):
    return jnp.broadcast_to(v[j : j + 1], (8, 128))


def eliminate(cols):
    sub = iota((8, 128), 0)
    cols = list(cols)
    invs = [jnp.where(sub == j, 1.0, 0.0).astype(jnp.float32) for j in range(8)]
    scales = None
    for j in range(8):
        scale = lax.rsqrt(pick(cols[j], j))
        scales = scale if scales is None else jnp.where(sub == j, scale, scales)
        if j == 7:
            break
        below = jnp.where(sub > j, cols[j], 0.0)
        square = scale * scale
        ratio = below * square
        cols[j + 1] = cols[j + 1] - (below * pick(cols[j + 1], j)) * square
        for m in range(j + 2, 8):
            cols[m] = cols[m] - ratio * pick(cols[m], j)
        for m in range(j):
            invs[m] = invs[m] - ratio * pick(invs[m], j)
        invs[j] = invs[j] - ratio
    return [v * scales for v in invs]


def thirds(x):
    high = x.astype(jnp.bfloat16).astype(jnp.float32)
    rest = x - high
    mid = rest.astype(jnp.bfloat16).astype(jnp.float32)
    return high, mid, rest - mid


def outer6(a, b):
    (ah, am, al), (bh, bm, bl) = a, b
    left = jnp.concatenate([ah, ah, am, am, ah, al], axis=0).astype(jnp.bfloat16)
    right = jnp.concatenate([bh, bm, bh, bm, bl, bh], axis=0).astype(jnp.bfloat16)
    return lax.dot_general(left, right, (((0,), (0,)), ((), ())), preferred_element_type=jnp.float32)


def factor_inverse(blocks, beside):
    count = len(blocks)
    beside = list(beside)
    due = [i * (count - 1) // len(beside) for i in range(len(beside))]
    mat = list(blocks)
    lane, sub = iota((8, 128), 1), iota((8, 128), 0)
    out = [jnp.where(lane == sub + 8 * i, 1.0, 0.0).astype(jnp.float32) for i in range(count)]

    def column(i, c):
        return jnp.broadcast_to(mat[i][:, c : c + 1], (8, 128))

    def apply(vectors, block):
        return tree([vectors[m] * pick(block, m) for m in range(8)])

    cols = [column(0, m) for m in range(8)]
    for k in range(count):
        invs = eliminate(cols)
        out[k] = apply(invs, out[k])
        if k + 1 == count:
            break
        done = apply(invs, mat[k])
        nxt = k + 1
        by = [column(nxt, 8 * k + m) for m in range(8)]
        factor = [tree([by[m] * pick(invs[m], j) for m in range(j + 1)]) for j in range(8)]
        if True:
            old = [column(nxt, 8 * nxt + m) for m in range(8)]
            cols = [old[m] - tree([factor[j] * pick(factor[j], m) for j in range(8)]) for m in range(8)]
        mat[nxt] = mat[nxt] - apply(factor, done)
        out[nxt] = out[nxt] - apply(factor, out[k])
        if not True:
            cols = [column(nxt, 8 * nxt + m) for m in range(8)]
        if nxt + 1 < count:
            both = thirds(jnp.concatenate([done, out[k]], axis=1))
            change = outer6([part[:, :128] for part in both], both)
            for i in range(nxt + 1, count):
                mat[i] = mat[i] - change[8 * i : 8 * i + 8, :128]
                out[i] = out[i] - change[8 * i : 8 * i + 8, 128:]
        for when, piece in zip(due, beside):
            if when == k:
                piece()
    return out


def dot6(a, b):
    (ah, am, al), (bh, bm, bl) = ([v.astype(jnp.bfloat16) for v in x] for x in (a, b))

    def part(u, v):
        return lax.dot_general(u, v, (((1,), (1,)), ((), ())), preferred_element_type=jnp.float32)

    def beside(u, v):
        return jnp.concatenate([u, v], axis=1)

    size = bh.shape[0]
    main = part(beside(ah, am), jnp.concatenate([beside(bh, bm), beside(bm, bh)], axis=0))
    return main[:, :size] + (main[:, size:] + part(beside(ah, al), beside(bl, bh)))


def remainder_kernel(
    count, sums_ref, late_ref, panel_ref, block_ref, over_hbm, coup_hbm,
    over_ref, coup_ref, panel2_ref, basis_ref, cross_ref, sem,
):
    steps = panel_ref.shape[0] // 128
    parts = 128 * steps // 512

    def early(t):
        row = jnp.concatenate([sums_ref[4 * t - 2 + b : 4 * t - 1 + b, :] for b in range(4)], axis=1)
        turned = pltpu.roll(jnp.broadcast_to(row, (128, 512)), 0, 1, stride=1, stride_axis=0)
        return turned[:, 256:512], turned[:, 128:384]

    half = jnp.concatenate([sums_ref[0:1, :], sums_ref[1:2, :], jnp.zeros((1, 128), jnp.float32)], axis=1)
    spun = pltpu.roll(jnp.broadcast_to(half, (128, 384)), 1, 1, stride=1, stride_axis=0)
    below_diagonal = spun[:, 256:384]
    gram_near = jnp.where(
        iota((128, 128), 0) >= iota((128, 128), 1), below_diagonal, jnp.transpose(below_diagonal)
    )
    gram11 = (gram_near + late_ref[:128, :128]) / count
    got = {}

    def gram_rest():
        got["gram21"] = thirds((spun[:, 128:256] + late_ref[128:, :128]) / count)
        got["gram22"] = (gram_near + late_ref[128:, 128:256]) / count

    def cross(t):
        def piece():
            top, low = early(t)
            cross_ref[:128, 256 * (t - 1) : 256 * t] = (top + late_ref[:128, 256 * t : 256 * t + 256]) / count
            cross_ref[128:, 256 * (t - 1) : 256 * t] = (low + late_ref[128:, 256 * t : 256 * t + 256]) / count

        return piece

    first = jnp.concatenate(
        factor_inverse(
            [gram11[8 * i : 8 * i + 8] for i in range(16)],
            [gram_rest] + [cross(1 + t) for t in range(2)],
        ),
        axis=0,
    )
    below = dot6(got["gram21"], thirds(first))
    below6 = thirds(below)
    schur = got["gram22"] - dot6(below6, below6)
    first2, below2 = split(first), split(below)

    def wide(i):
        return slice(256 * i, 256 * i + 256)

    def couple(i):
        def piece():
            coup_ref[:128, wide(i)] = dot3(first2, split(cross_ref[:128, wide(i)]))

        return piece

    def couple_rest(i):
        def piece():
            cross_ref[128:, wide(i)] = cross_ref[128:, wide(i)] - dot3(below2, split(coup_ref[:128, wide(i)]))

        return piece

    def upper(s):
        return slice(512 * s, 512 * s + 512)

    def orthogonalize(s):
        def piece():
            basis_ref[upper(s), :] = dot3(split(panel_ref[upper(s), :128]), first2, True)

        return piece

    def orthogonalize_rest(s):
        def piece():
            panel2_ref[upper(s), :] = panel_ref[upper(s), 128:] - dot3(split(basis_ref[upper(s), :]), below2, True)

        return piece

    def project(s, i):
        def piece():
            change = dot3(split(basis_ref[upper(s), :]), split(coup_ref[:128, wide(i)]))
            over_ref[upper(s), wide(i)] = block_ref[upper(s), wide(i)] - change

        return piece

    second = jnp.concatenate(
        factor_inverse(
            [schur[8 * i : 8 * i + 8] for i in range(16)],
            [couple(i) for i in range(2)]
            + [orthogonalize(s) for s in range(parts)]
            + [project(s, i) for i in range(2) for s in range(parts)]
            + [couple_rest(i) for i in range(2)]
            + [orthogonalize_rest(s) for s in range(parts)],
        ),
        axis=0,
    )
    second2 = split(second)
    basis2 = dot3(split(panel2_ref[...]), second2, True)
    basis2s = split(basis2)
    out = []
    for i in (1, 0):
        coup2 = dot3(second2, split(cross_ref[128:, wide(i)]))
        coup_ref[128:, wide(i)] = coup2
        if i == 0:
            out.append(pltpu.make_async_copy(coup_ref, coup_hbm, sem.at[3]))
            out[-1].start()
        coup2s = split(coup2)
        height = over_ref.shape[0] // (2 - i)
        for part in range(2 - i):
            rows = slice(height * part, height * part + height)
            change = dot3([v[rows] for v in basis2s], coup2s)
            over_ref[rows, wide(i)] = over_ref[rows, wide(i)] - change
            if i == 0:

                @pl.when(lax.axis_index("col") == 0)
                def _():
                    over_ref[rows, :128] = basis_ref[rows, :]
                    over_ref[rows, 128:WIDE] = basis2[rows]

            out.append(
                pltpu.make_async_copy(over_ref.at[rows, wide(i)], over_hbm.at[rows, wide(i)], sem.at[2 * i + part])
            )
            out[-1].start()
    for copy in out:
        copy.wait()


def remainder(sums, late, panel, block, count):
    rows, f32 = panel.shape[0], jnp.float32
    anywhere = pl.BlockSpec(memory_space=pl.ANY)
    return pl.pallas_call(
        functools.partial(remainder_kernel, count),
        name="remainder",
        out_shape=(jax.ShapeDtypeStruct((rows, 512), f32), jax.ShapeDtypeStruct((WIDE, 512), f32)),
        in_specs=[VM, VM, VM, VM],
        out_specs=(anywhere, anywhere),
        scratch_shapes=[
            pltpu.VMEM((rows, 512), f32),
            pltpu.VMEM((WIDE, 512), f32),
            pltpu.VMEM((rows, 128), f32),
            pltpu.VMEM((rows, 128), f32),
            pltpu.VMEM((WIDE, 512), f32),
            pltpu.SemaphoreType.DMA((4,)),
        ],
        compiler_params=pltpu.CompilerParams(vmem_limit_bytes=24 * 2**20),
    )(sums, late, panel, block)


def solution(mesh):
    slabs, cols = mesh.shape["row"] // SLAB, mesh.shape["col"]

    def body(traces):
        count = traces.shape[1] * slabs * SLAB
        held = pltpu.with_memory_space_constraint(traces, pltpu.HBM)
        return remainder(*lag_sums(held, slabs, cols), count)

    return jax.shard_map(
        body,
        mesh=mesh,
        in_specs=(P("col", "row"),),
        out_specs=(P("row", "col"), P(None, "col")),
        check_vma=False,
    )
```

```python
import functools

import jax
import jax.numpy as jnp
from jax import lax
from jax.experimental import pallas as pl
from jax.experimental.pallas import tpu as pltpu
from jax.sharding import PartitionSpec as P

TAPS = 256
WIDE = 256
SLAB = 4
MESH = pl.DeviceIdType.MESH
HIGHEST = lax.Precision.HIGHEST
VM = pl.BlockSpec(memory_space=pltpu.VMEM)


def dot(a, b, da=1, db=0):
    return lax.dot_general(
        a, b, (((da,), (db,)), ((), ())), precision=HIGHEST, preferred_element_type=jnp.float32
    )


def iota(shape, axis):
    return lax.broadcasted_iota(jnp.int32, shape, axis)


def anti_identity():
    return jnp.where(iota((128, 128), 0) + iota((128, 128), 1) == 127, 1.0, 0.0).astype(jnp.float32)


def lag_kernel(
    slabs, cols,
    x_hbm, sums_ref, late_ref, panel_ref, block_ref,
    x_ref, ext_ref, mine, own0, slab0, slabc, before0, after0, beforec, late0, latec, lags,
    local_sem, send_x, recv_x, send_0, recv_0, send_hc, recv_hc,
    send_s0, recv_s0, send_hb, recv_hb, send_ha, recv_ha, send_t, recv_t, send_l, recv_l, hello,
):
    fetch = pltpu.make_async_copy(x_hbm, x_ref, local_sem.at[1])
    fetch.start()
    row, col = lax.axis_index("row"), lax.axis_index("col")
    z, y = row // SLAB, row % SLAB
    per = x_ref.shape[1] // 128
    first, last = y == 0, y == SLAB - 1
    has_before, has_after = z > 0, z < slabs - 1
    in_tail = z == slabs - 1

    def at(zz, yy, cc):
        return (zz * SLAB + yy, cc)

    def around(k):
        return at((z + k + slabs) % slabs, y, col)

    def remote(src, dst, send, recv, where):
        return pltpu.make_async_remote_copy(
            src_ref=src, dst_ref=dst, send_sem=send, recv_sem=recv, device_id=where, device_id_type=MESH
        )

    barrier = pltpu.get_barrier_semaphore()

    def greet(where):
        pl.semaphore_signal(barrier, inc=1, device_id=where, device_id_type=MESH)

    greet(around(1))
    greet(around(-1))

    @pl.when(last & has_after)
    def _():
        for k in range(SLAB):
            greet(at(z + 1, k, col))

    @pl.when(first & has_before)
    def _():
        for k in range(SLAB):
            greet(at(z - 1, k, col))

    @pl.when(has_before)
    def _():
        greet(at(z - 1, SLAB - 1, col))

    @pl.when(has_after)
    def _():
        greet(at(z + 1, 0, col))

    @pl.when(col == 0)
    def _():
        for k in range(1, cols):
            greet(at(z, y, k))

    @pl.when(col != 0)
    def _():
        greet(at(z, y, 0))

    for k in range(1, SLAB):
        greet(at(z, (y + k) % SLAB, col))

    def yes(flag):
        return jnp.where(flag, 1, 0)

    expected = (
        2 + SLAB - 1 + yes(col != 0) + (cols - 1) * yes(col == 0)
        + SLAB * yes(last & has_after) + SLAB * yes(first & has_before)
        + yes(has_before) + yes(has_after)
    )

    @pl.when(z == 0)
    def _():
        before0[...] = jnp.zeros_like(before0)
        beforec[...] = jnp.zeros_like(beforec)

    @pl.when(in_tail)
    def _():
        after0[...] = jnp.zeros_like(after0)

    fetch.wait()
    plain = jnp.concatenate(
        [x_ref[t : t + 1, 128 * b : 128 * b + 128] for t in range(2) for b in range(per)], axis=0
    )
    turned = dot(plain, anti_identity())
    mine[...] = turned
    slabc[y] = turned

    @pl.when(col == 0)
    def _():
        own0[:per, :] = plain[:per]
        own0[per:, :] = turned[:per]

    pl.semaphore_wait(barrier, expected)

    @pl.when(col == 0)
    def _():
        for k in range(1, cols):
            remote(own0, own0, send_0.at[k], recv_0.at[0], at(z, y, k)).start()

    for k in range(1, SLAB):
        remote(mine, slabc.at[y], send_x.at[k], recv_x.at[y], at(z, (y + k) % SLAB, col)).start()

    @pl.when(last & has_after)
    def _():
        remote(mine, beforec, send_hc.at[0], recv_hc.at[0], at(z + 1, 0, col)).start()

    reach = [r for r in (1, 2, 4, 8, 16) if 4 * r <= slabs]

    def tell(i):
        for k in (reach[i], -reach[i]):
            pl.semaphore_signal(hello.at[i], inc=1, device_id=around(k), device_id_type=MESH)

    if reach:
        tell(0)
    if len(reach) > 1:
        pl.semaphore_wait(hello.at[0], 2)
        tell(1)

    @pl.when(col != 0)
    def _():
        remote(own0, own0, send_0.at[0], recv_0.at[0], at(z, y, 0)).wait_recv()

    keep_0 = pltpu.make_async_copy(own0, slab0.at[y], local_sem.at[0])
    keep_0.start()
    for k in range(1, SLAB):
        remote(own0, slab0.at[y], send_s0.at[k], recv_s0.at[y], at(z, (y + k) % SLAB, col)).start()

    @pl.when(last & has_after)
    def _():
        for k in range(SLAB):
            remote(own0, before0, send_hb.at[k], recv_hb.at[0], at(z + 1, k, col)).start()

    @pl.when(first & has_before)
    def _():
        for k in range(SLAB):
            remote(own0.at[0:2], after0, send_ha.at[k], recv_ha.at[0], at(z - 1, k, col)).start()

    for i in range(2, len(reach)):
        pl.semaphore_wait(hello.at[i - 1], 2)
        tell(i)

    keep_0.wait()
    for k in range(1, SLAB):
        other = (y + k) % SLAB
        remote(mine, slabc.at[other], send_x.at[k], recv_x.at[other], at(z, other, col)).wait_recv()
        remote(own0, slab0.at[other], send_s0.at[k], recv_s0.at[other], at(z, other, col)).wait_recv()

    @pl.when(has_before)
    def _():
        remote(own0, before0, send_hb.at[0], recv_hb.at[0], at(z, y, col)).wait_recv()

    @pl.when(has_after)
    def _():
        remote(own0.at[0:2], after0, send_ha.at[0], recv_ha.at[0], at(z, y, col)).wait_recv()

    def all_came():
        if reach:
            pl.semaphore_wait(hello.at[len(reach) - 1], 2)

    def tails(k):
        return (
            remote(slab0.at[SLAB - 1, per - 2 : per], late0, send_t.at[0, k], recv_t.at[0], around(k)),
            remote(slabc.at[SLAB - 1, per - 2 : per], latec.at[0], send_t.at[1, k], recv_t.at[1], around(k)),
            remote(slabc.at[SLAB - 1, 2 * per - 2 :], latec.at[1], send_t.at[2, k], recv_t.at[2], around(k)),
        )

    @pl.when(in_tail)
    def _():
        all_came()

        @pl.loop(1, slabs)
        def _(k):
            for copy in tails(k):
                copy.start()

        late0[...] = slab0[SLAB - 1, per - 2 : per]
        latec[0] = slabc[SLAB - 1, per - 2 : per]
        latec[1] = slabc[SLAB - 1, 2 * per - 2 :]

    count = SLAB * per
    ext0 = jnp.concatenate([before0[per - 2 : per, :]] + [slab0[j, :per, :] for j in range(SLAB)] + [after0[...]], axis=0)
    wide0 = jnp.concatenate([ext0[k : k + count] for k in range(5)], axis=1)
    place = iota((count, 640), 0) * 128 + iota((count, 640), 1) - 256
    late = count * 128 - (TAPS - 1)
    wide0_early = jnp.where(in_tail & (place >= late), 0.0, wide0)
    right = jnp.concatenate([wide0, wide0_early[count - 8 :]], axis=0)
    at_late = in_tail & (iota((count, 128), 0) * 128 + 127 - iota((count, 128), 1) >= late)
    lefts = []
    for t in range(3):
        if t == 0:
            group = jnp.concatenate([slab0[j, per:, :] for j in range(SLAB)], axis=0)
        else:
            group = jnp.concatenate([slabc[j, per * (t - 1) : per * t, :] for j in range(SLAB)], axis=0)
        lefts.append(
            jnp.concatenate([jnp.where(at_late, 0.0, group), jnp.where(at_late, group, 0.0)[count - 8 :]], axis=0)
        )
    table = outer6(thirds(jnp.concatenate(lefts, axis=1)), thirds(right))
    for t in range(3):
        skewed = pltpu.roll(table[128 * t : 128 * t + 128], min(t, 1), 1, stride=1, stride_axis=0)
        summed = jnp.sum(skewed, axis=0, keepdims=True)
        at_row = max(4 * t - 2, 0)
        for b in range(2 if t == 0 else 4):
            lags[z, at_row + b : at_row + b + 1, :] = summed[:, 128 + 128 * b : 256 + 128 * b]

    def exchange(k):
        return remote(lags.at[z], lags.at[z], send_l.at[k], recv_l.at[0], around(k))

    pl.when(z < slabs - 1)(all_came)

    for k in sorted(range(1, slabs), key=lambda k: -min(k, slabs - k)):
        exchange(k).start()

    reach_back = per + 2
    ext_ref[2:reach_back, :] = own0[per:, :]
    for t in range(2):
        ext_ref[reach_back * (t + 1) + 2 : reach_back * (t + 2), :] = mine[per * t : per * t + per, :]

    @pl.when(first)
    def _():
        @pl.when(has_before)
        def _():
            remote(mine, beforec, send_hc.at[0], recv_hc.at[0], at(z, y, col)).wait_recv()

        ext_ref[0:2, :] = before0[2 * per - 2 :, :]
        for t in range(2):
            ext_ref[reach_back * (t + 1) : reach_back * (t + 1) + 2, :] = beforec[per * t + per - 2 : per * t + per, :]

    @pl.when(y > 0)
    def _():
        before = (y + SLAB - 1) % SLAB
        ext_ref[0:2, :] = slab0[before, 2 * per - 2 :, :]
        for t in range(2):
            ext_ref[reach_back * (t + 1) : reach_back * (t + 1) + 2, :] = slabc[before, per * t + per - 2 : per * t + per, :]

    for t in range(3):
        line = jnp.concatenate(
            [ext_ref[reach_back * t + b : reach_back * t + b + 1, :] for b in reversed(range(reach_back))], axis=1
        )
        spun = pltpu.roll(jnp.broadcast_to(line, (128, 128 * reach_back)), 1, 1, stride=1, stride_axis=0)
        for k in range(2):
            for s in range(per):
                block = spun[:, 512 + 128 * (k - s) : 640 + 128 * (k - s)]
                if t == 0:
                    panel_ref[128 * s : 128 * s + 128, 128 * k : 128 * k + 128] = block
                else:
                    block_ref[128 * s : 128 * s + 128, 256 * (t - 1) + 128 * k : 256 * (t - 1) + 128 * k + 128] = block

    @pl.when(z < slabs - 1)
    def _():
        for copy in tails(0):
            copy.wait_recv()

    ends = jnp.concatenate([latec[0], latec[1], jnp.zeros((4, 128), jnp.float32)], axis=0)
    forward = dot(ends, anti_identity())

    def late_rows(t):
        rows = late0[...] if t == 0 else forward[2 * t - 2 : 2 * t]
        tail = jnp.where(iota((1, TAPS), 1) == 0, 0.0, jnp.concatenate([rows[0:1], rows[1:2]], axis=1))
        line = jnp.concatenate([jnp.zeros((1, 128), jnp.float32), tail], axis=1)
        spun = pltpu.roll(jnp.broadcast_to(line, (128, 384)), 0, 1, stride=1, stride_axis=0)
        return spun[:, 128:256], spun[:, 256:384]

    near0, far0 = late_rows(0)
    near6, far6 = thirds(near0), thirds(far0)
    near_near = dot6(near6, near6)
    late_ref[:128, :128] = near_near + dot6(far6, far6)
    late_ref[128:, :128] = dot6(near6, far6)
    late_ref[128:, 128:256] = near_near
    near_a, far_a = split(near0), split(far0)
    for t in (1, 2):
        near_c, far_c = (split(v) for v in late_rows(t))
        same = dot3(near_a, near_c, True)
        late_ref[:128, 256 * t : 256 * t + 128] = same + dot3(far_a, far_c, True)
        late_ref[:128, 256 * t + 128 : 256 * t + 256] = dot3(far_a, near_c, True)
        late_ref[128:, 256 * t : 256 * t + 128] = dot3(near_a, far_c, True)
        late_ref[128:, 256 * t + 128 : 256 * t + 256] = same

    @pl.when(col == 0)
    def _():
        for k in range(1, cols):
            remote(own0, own0, send_0.at[k], recv_0.at[0], at(z, y, k)).wait_send()

    for k in range(1, SLAB):
        other = (y + k) % SLAB
        remote(mine, slabc.at[y], send_x.at[k], recv_x.at[y], at(z, other, col)).wait_send()
        remote(own0, slab0.at[y], send_s0.at[k], recv_s0.at[y], at(z, other, col)).wait_send()

    @pl.when(last & has_after)
    def _():
        remote(mine, beforec, send_hc.at[0], recv_hc.at[0], at(z + 1, 0, col)).wait_send()
        for k in range(SLAB):
            remote(own0, before0, send_hb.at[k], recv_hb.at[0], at(z + 1, k, col)).wait_send()

    @pl.when(first & has_before)
    def _():
        for k in range(SLAB):
            remote(own0.at[0:2], after0, send_ha.at[k], recv_ha.at[0], at(z - 1, k, col)).wait_send()

    @pl.when(in_tail)
    def _():
        @pl.loop(1, slabs)
        def _(k):
            for copy in tails(k):
                copy.wait_send()

    @pl.loop(1, slabs)
    def _(k):
        exchange(k).wait_send()

    others = lags.at[pl.ds(0, slabs - 1)]
    remote(others, others, send_l.at[0], recv_l.at[0], around(1)).wait_recv()

    sums_ref[...] = tree([lags[k] for k in range(slabs)])


def lag_sums(traces, slabs, cols):
    rows = traces.shape[1]
    per = rows // 128
    f32, dma = jnp.float32, pltpu.SemaphoreType.DMA
    return pl.pallas_call(
        functools.partial(lag_kernel, slabs, cols),
        name="lag_sums",
        out_shape=(
            jax.ShapeDtypeStruct((10, 128), f32),
            jax.ShapeDtypeStruct((WIDE, WIDE + 2 * TAPS), f32),
            jax.ShapeDtypeStruct((rows, WIDE), f32),
            jax.ShapeDtypeStruct((rows, 2 * TAPS), f32),
        ),
        in_specs=[pl.BlockSpec(memory_space=pltpu.HBM)],
        out_specs=(VM, VM, VM, VM),
        scratch_shapes=[
            pltpu.VMEM((2, rows), f32),
            pltpu.VMEM((3 * (per + 2), 128), f32),
            pltpu.VMEM((2 * per, 128), f32),
            pltpu.VMEM((2 * per, 128), f32),
            pltpu.VMEM((SLAB, 2 * per, 128), f32),
            pltpu.VMEM((SLAB, 2 * per, 128), f32),
            pltpu.VMEM((2 * per, 128), f32),
            pltpu.VMEM((2, 128), f32),
            pltpu.VMEM((2 * per, 128), f32),
            pltpu.VMEM((2, 128), f32),
            pltpu.VMEM((2, 2, 128), f32),
            pltpu.VMEM((slabs, 10, 128), f32),
            dma((2,)),
            dma((SLAB,)), dma((SLAB,)),
            dma((cols,)), dma((1,)),
            dma((1,)), dma((1,)),
            dma((SLAB,)), dma((SLAB,)),
            dma((SLAB,)), dma((1,)),
            dma((SLAB,)), dma((1,)),
            dma((3, slabs)), dma((3,)),
            dma((slabs,)), dma((slabs,)),
            pltpu.SemaphoreType.REGULAR((5,)),
        ],
        compiler_params=pltpu.CompilerParams(
            collective_id=0, has_side_effects=True, vmem_limit_bytes=12 * 2**20
        ),
    )(traces)


def split(x):
    high = x.astype(jnp.bfloat16)
    return high, (x - high.astype(jnp.float32)).astype(jnp.bfloat16)


def dot3(a, b, nt=False):
    (ah, al), (bh, bl) = a, b
    left = jnp.concatenate([ah, al, ah], axis=1)
    right = jnp.concatenate([bh, bh, bl], axis=1 if nt else 0)
    return lax.dot_general(
        left, right, (((1,), (1 if nt else 0,)), ((), ())), preferred_element_type=jnp.float32
    )


def tree(terms):
    while len(terms) > 1:
        terms = [terms[i] + terms[i + 1] if i + 1 < len(terms) else terms[i] for i in range(0, len(terms), 2)]
    return terms[0]


def pick(v, j):
    return jnp.broadcast_to(v[j : j + 1], (8, 128))


def eliminate(cols):
    sub = iota((8, 128), 0)
    cols = list(cols)
    invs = [jnp.where(sub == j, 1.0, 0.0).astype(jnp.float32) for j in range(8)]
    scales = None
    for j in range(8):
        scale = lax.rsqrt(pick(cols[j], j))
        scales = scale if scales is None else jnp.where(sub == j, scale, scales)
        if j == 7:
            break
        below = jnp.where(sub > j, cols[j], 0.0)
        square = scale * scale
        ratio = below * square
        cols[j + 1] = cols[j + 1] - (below * pick(cols[j + 1], j)) * square
        for m in range(j + 2, 8):
            cols[m] = cols[m] - ratio * pick(cols[m], j)
        for m in range(j):
            invs[m] = invs[m] - ratio * pick(invs[m], j)
        invs[j] = invs[j] - ratio
    return [v * scales for v in invs]


def thirds(x):
    high = x.astype(jnp.bfloat16).astype(jnp.float32)
    rest = x - high
    mid = rest.astype(jnp.bfloat16).astype(jnp.float32)
    return high, mid, rest - mid


def outer6(a, b):
    (ah, am, al), (bh, bm, bl) = a, b
    left = jnp.concatenate([ah, ah, am, am, ah, al], axis=0).astype(jnp.bfloat16)
    right = jnp.concatenate([bh, bm, bh, bm, bl, bh], axis=0).astype(jnp.bfloat16)
    return lax.dot_general(left, right, (((0,), (0,)), ((), ())), preferred_element_type=jnp.float32)


def factor_inverse(blocks, beside):
    count = len(blocks)
    beside = list(beside)
    due = [i * (count - 1) // len(beside) for i in range(len(beside))]
    mat = list(blocks)
    lane, sub = iota((8, 128), 1), iota((8, 128), 0)
    out = [jnp.where(lane == sub + 8 * i, 1.0, 0.0).astype(jnp.float32) for i in range(count)]

    def column(i, c):
        return jnp.broadcast_to(mat[i][:, c : c + 1], (8, 128))

    def apply(vectors, block):
        return tree([vectors[m] * pick(block, m) for m in range(8)])

    cols = [column(0, m) for m in range(8)]
    for k in range(count):
        invs = eliminate(cols)
        out[k] = apply(invs, out[k])
        if k + 1 == count:
            break
        done = apply(invs, mat[k])
        nxt = k + 1
        by = [column(nxt, 8 * k + m) for m in range(8)]
        factor = [tree([by[m] * pick(invs[m], j) for m in range(j + 1)]) for j in range(8)]
        if True:
            old = [column(nxt, 8 * nxt + m) for m in range(8)]
            cols = [old[m] - tree([factor[j] * pick(factor[j], m) for j in range(8)]) for m in range(8)]
        mat[nxt] = mat[nxt] - apply(factor, done)
        out[nxt] = out[nxt] - apply(factor, out[k])
        if not True:
            cols = [column(nxt, 8 * nxt + m) for m in range(8)]
        if nxt + 1 < count:
            both = thirds(jnp.concatenate([done, out[k]], axis=1))
            change = outer6([part[:, :128] for part in both], both)
            for i in range(nxt + 1, count):
                mat[i] = mat[i] - change[8 * i : 8 * i + 8, :128]
                out[i] = out[i] - change[8 * i : 8 * i + 8, 128:]
        for when, piece in zip(due, beside):
            if when == k:
                piece()
    return out


def dot6(a, b):
    (ah, am, al), (bh, bm, bl) = ([v.astype(jnp.bfloat16) for v in x] for x in (a, b))

    def part(u, v):
        return lax.dot_general(u, v, (((1,), (1,)), ((), ())), preferred_element_type=jnp.float32)

    def beside(u, v):
        return jnp.concatenate([u, v], axis=1)

    size = bh.shape[0]
    main = part(beside(ah, am), jnp.concatenate([beside(bh, bm), beside(bm, bh)], axis=0))
    return main[:, :size] + (main[:, size:] + part(beside(ah, al), beside(bl, bh)))


def remainder_kernel(
    count, sums_ref, late_ref, panel_ref, block_ref, over_hbm, coup_hbm,
    over_ref, coup_ref, panel2_ref, basis_ref, cross_ref, sem,
):
    steps = panel_ref.shape[0] // 128
    parts = 128 * steps // 512

    def early(t):
        row = jnp.concatenate([sums_ref[4 * t - 2 + b : 4 * t - 1 + b, :] for b in range(4)], axis=1)
        turned = pltpu.roll(jnp.broadcast_to(row, (128, 512)), 0, 1, stride=1, stride_axis=0)
        return turned[:, 256:512], turned[:, 128:384]

    half = jnp.concatenate([sums_ref[0:1, :], sums_ref[1:2, :], jnp.zeros((1, 128), jnp.float32)], axis=1)
    spun = pltpu.roll(jnp.broadcast_to(half, (128, 384)), 1, 1, stride=1, stride_axis=0)
    below_diagonal = spun[:, 256:384]
    gram_near = jnp.where(
        iota((128, 128), 0) >= iota((128, 128), 1), below_diagonal, jnp.transpose(below_diagonal)
    )
    gram11 = (gram_near + late_ref[:128, :128]) / count
    got = {}

    def gram_rest():
        got["gram21"] = thirds((spun[:, 128:256] + late_ref[128:, :128]) / count)
        got["gram22"] = (gram_near + late_ref[128:, 128:256]) / count

    def cross(t):
        def piece():
            top, low = early(t)
            cross_ref[:128, 256 * (t - 1) : 256 * t] = (top + late_ref[:128, 256 * t : 256 * t + 256]) / count
            cross_ref[128:, 256 * (t - 1) : 256 * t] = (low + late_ref[128:, 256 * t : 256 * t + 256]) / count

        return piece

    first = jnp.concatenate(
        factor_inverse(
            [gram11[8 * i : 8 * i + 8] for i in range(16)],
            [gram_rest] + [cross(1 + t) for t in range(2)],
        ),
        axis=0,
    )
    below = dot6(got["gram21"], thirds(first))
    below6 = thirds(below)
    schur = got["gram22"] - dot6(below6, below6)
    first2, below2 = split(first), split(below)

    def wide(i):
        return slice(256 * i, 256 * i + 256)

    def couple(i):
        def piece():
            coup_ref[:128, wide(i)] = dot3(first2, split(cross_ref[:128, wide(i)]))

        return piece

    def couple_rest(i):
        def piece():
            cross_ref[128:, wide(i)] = cross_ref[128:, wide(i)] - dot3(below2, split(coup_ref[:128, wide(i)]))

        return piece

    def upper(s):
        return slice(512 * s, 512 * s + 512)

    def orthogonalize(s):
        def piece():
            basis_ref[upper(s), :] = dot3(split(panel_ref[upper(s), :128]), first2, True)

        return piece

    def orthogonalize_rest(s):
        def piece():
            panel2_ref[upper(s), :] = panel_ref[upper(s), 128:] - dot3(split(basis_ref[upper(s), :]), below2, True)

        return piece

    def project(s, i):
        def piece():
            change = dot3(split(basis_ref[upper(s), :]), split(coup_ref[:128, wide(i)]))
            over_ref[upper(s), wide(i)] = block_ref[upper(s), wide(i)] - change

        return piece

    second = jnp.concatenate(
        factor_inverse(
            [schur[8 * i : 8 * i + 8] for i in range(16)],
            [couple(i) for i in range(2)]
            + [orthogonalize(s) for s in range(parts)]
            + [project(s, i) for i in range(2) for s in range(parts)]
            + [couple_rest(i) for i in range(2)]
            + [orthogonalize_rest(s) for s in range(parts)],
        ),
        axis=0,
    )
    second2 = split(second)
    basis2 = dot3(split(panel2_ref[...]), second2, True)
    basis2s = split(basis2)
    out = []
    for i in (1, 0):
        coup2 = dot3(second2, split(cross_ref[128:, wide(i)]))
        coup_ref[128:, wide(i)] = coup2
        if i == 0:
            out.append(pltpu.make_async_copy(coup_ref, coup_hbm, sem.at[2]))
            out[-1].start()
        over_ref[:, wide(i)] = over_ref[:, wide(i)] - dot3(basis2s, split(coup2))
        if i == 0:

            @pl.when(lax.axis_index("col") == 0)
            def _():
                over_ref[:, :128] = basis_ref[...]
                over_ref[:, 128:WIDE] = basis2

        out.append(pltpu.make_async_copy(over_ref.at[:, wide(i)], over_hbm.at[:, wide(i)], sem.at[i]))
        out[-1].start()
    for copy in out:
        copy.wait()


def remainder(sums, late, panel, block, count):
    rows, f32 = panel.shape[0], jnp.float32
    anywhere = pl.BlockSpec(memory_space=pl.ANY)
    return pl.pallas_call(
        functools.partial(remainder_kernel, count),
        name="remainder",
        out_shape=(jax.ShapeDtypeStruct((rows, 512), f32), jax.ShapeDtypeStruct((WIDE, 512), f32)),
        in_specs=[VM, VM, VM, VM],
        out_specs=(anywhere, anywhere),
        scratch_shapes=[
            pltpu.VMEM((rows, 512), f32),
            pltpu.VMEM((WIDE, 512), f32),
            pltpu.VMEM((rows, 128), f32),
            pltpu.VMEM((rows, 128), f32),
            pltpu.VMEM((WIDE, 512), f32),
            pltpu.SemaphoreType.DMA((3,)),
        ],
        compiler_params=pltpu.CompilerParams(vmem_limit_bytes=24 * 2**20),
    )(sums, late, panel, block)


def solution(mesh):
    slabs, cols = mesh.shape["row"] // SLAB, mesh.shape["col"]

    def body(traces):
        count = traces.shape[1] * slabs * SLAB
        held = pltpu.with_memory_space_constraint(traces, pltpu.HBM)
        return remainder(*lag_sums(held, slabs, cols), count)

    return jax.shard_map(
        body,
        mesh=mesh,
        in_specs=(P("col", "row"),),
        out_specs=(P("row", "col"), P(None, "col")),
        check_vma=False,
    )
```
